32 devices in a mesh: dp: 4 (over z), ctx: 2 (over x), tp: 4 (over y, core).
Axes of the slice: x: 2, y: 2, z: 4, core: 2. Of those that a mesh axis runs over, the one named last changes fastest.
Arguments:
- q_long: bfloat16 [4, 512, 4096], P('dp', 'ctx', 'tp'), may hold values from -24 to 24
- long_key_value: bfloat16 [4, 2, 512, 512], P('dp', None, 'ctx', 'tp'), may hold values from -24 to 24
- q_short: bfloat16 [8, 128, 4096], P(('dp', 'ctx'), None, 'tp'), may hold values from -24 to 24
- short_key_value: bfloat16 [8, 2, 128, 512], P(('dp', 'ctx'), None, None, 'tp'), may hold values from -24 to 24
- doc_ids: int32 [8, 128], P(('dp', 'ctx')), may hold values from 0 to 15, as said below
- live_counts: int32 [8], P(('dp', 'ctx')), may hold values from 64 to 128, as said below
- rescale: float32 [64], replicated, may hold values from 1 to 32
- output_weight: bfloat16 [4, 1024, 8192], P('tp', 'dp', 'ctx'), may hold values from -0.09375 to 0.09375
Outputs:
- projected: bfloat16 [4, 704, 8192], P('dp', 'tp', 'ctx')
The draws below stay inside these ranges and needn't reach their ends.
Inputs may be any that keep to these rules, and one draw needn't show every extreme that they name: `doc_ids`: along each slab the document number starts at 0, never falls, rises by at most one, and rises only at slots that are multiples of 8. `live_counts`: multiples of 8; the counts of the slabs of one document group sum to 96 times their number.
All inputs are finite; a program needn't handle non-finite values.
Results may differ from the reference program's by a relative error of at most 0.009.
Values may be sent and summed in bfloat16 or wider, within the bound.
No kernel may reach another device: no remote copies, remote signals or barrier semaphores. Data moves between devices by JAX's collectives and lax.ppermute only.
A program may use at most 128 MiB of HBM per device.

```python
import math
import jax
import jax.numpy as jnp
from jax import lax

MODEL_WIDTH = 8192
HEAD_WIDTH = 128
QUERIES_PER_KEY = 8
LONG_DEV = 256
SLAB_SLOTS = 128
KEY_HEADS = 4
QUERY_HEADS = 32
LONG_DOC_ROWS = 512
SLAB_COUNT = 8
SLOT = 384
SHORT_LIVE = 96
GROUP_TOK = 704
N_DP = 4
N_CTX = 2


def drawn_draw(key, leading_axes, token_rows, salt):
    base_key = jax.random.fold_in(key, salt)
    query_random_key, pairing_key = jax.random.split(base_key, 2)
    query_tensor = 1.3 * jnp.clip(jax.random.normal(query_random_key, (leading_axes, token_rows, KEY_HEADS, QUERIES_PER_KEY, HEAD_WIDTH), jnp.float32), -5.0, 5.0)
    scale_factors = jnp.array([1.3, 1.0], jnp.float32).reshape(1, 2, 1, 1, 1)
    row_pairs = scale_factors * jnp.clip(jax.random.normal(pairing_key, (leading_axes, 2, token_rows, KEY_HEADS, HEAD_WIDTH), jnp.float32), -5.0, 5.0)
    return (query_tensor.reshape(leading_axes, token_rows, KEY_HEADS * QUERIES_PER_KEY * HEAD_WIDTH), row_pairs.reshape(leading_axes, 2, token_rows, KEY_HEADS * HEAD_WIDTH))


def draw_q_long(key, part):
    return drawn_draw(key, N_DP, LONG_DOC_ROWS, 11)[0].astype(jnp.bfloat16)


def draw_long_key_value(key, part):
    return drawn_draw(key, N_DP, LONG_DOC_ROWS, 11)[1].astype(jnp.bfloat16)


def draw_q_short(key, part):
    return drawn_draw(key, SLAB_COUNT, SLAB_SLOTS, 12)[0].astype(jnp.bfloat16)


def draw_short_key_value(key, part):
    return drawn_draw(key, SLAB_COUNT, SLAB_SLOTS, 12)[1].astype(jnp.bfloat16)


def draw_doc_ids(key, part):
    block_count = SLAB_SLOTS // 8
    flag_key = jax.random.fold_in(key, 21)
    flags = jax.random.randint(flag_key, (SLAB_COUNT, block_count), 0, 4) == 0
    flags = flags.at[0].set(True)
    flags = flags.at[:, 0].set(False)
    block_ids = jnp.cumsum(flags.astype(jnp.int32), axis=1)
    return jnp.repeat(block_ids, 8, axis=1).astype(jnp.int32)


def draw_live_counts(key, part):
    reach = SLAB_SLOTS // 32
    step_key, order_key = jax.random.split(jax.random.fold_in(key, 31))
    steps_drawn = jax.random.randint(step_key, (N_DP, N_CTX // 2), 0, reach + 1)
    steps_drawn = steps_drawn.at[:, 0].set(reach)
    paired = jnp.stack([SHORT_LIVE + 8 * steps_drawn, SHORT_LIVE - 8 * steps_drawn], axis=2).reshape(N_DP, N_CTX)
    orders = jax.vmap(lambda group_key: jax.random.permutation(group_key, N_CTX))(jax.random.split(order_key, N_DP))
    counts = jnp.take_along_axis(paired, orders, axis=1)
    return counts.reshape(SLAB_COUNT).astype(jnp.int32)


def level_of(stream_key, dims, cuts, least, high):
    def one(axis_at, parts):
        heights = jax.random.uniform(jax.random.fold_in(jax.random.fold_in(stream_key, 6), axis_at), (parts,), jnp.float32, least / len(cuts), high / len(cuts))
        return jnp.repeat(jnp.exp(heights), dims[axis_at] // parts).reshape((-1,) + (1,) * (len(dims) - axis_at - 1))

    gain = one(*cuts[0])
    for cut in cuts[1:]:
        gain = gain * one(*cut)
    return gain


def scatter_about(key, dims, width, most, pieces=(), kind=jnp.bfloat16):
    level = level_of(key, dims, pieces, -0.22, 0.18) if pieces else 1.0
    result = jax.random.normal(key, dims, jnp.float32) * width * level
    return jnp.minimum(jnp.maximum(result, -most), most).astype(kind)


def setup_inputs(seed: int = 0) -> dict:
    arg_keys = jax.random.split(jax.random.key(seed), 9)
    q_long = draw_q_long(jax.random.fold_in(arg_keys[8], 71), 0)
    long_key_value = draw_long_key_value(jax.random.fold_in(arg_keys[8], 71), 0)
    q_short = draw_q_short(jax.random.fold_in(arg_keys[8], 71), 0)
    short_key_value = draw_short_key_value(jax.random.fold_in(arg_keys[8], 71), 0)
    doc_ids = draw_doc_ids(jax.random.fold_in(arg_keys[8], 71), 0)
    live_counts = draw_live_counts(jax.random.fold_in(arg_keys[8], 71), 0)
    rescale = jnp.clip(jnp.exp(jax.random.uniform(arg_keys[6], (HEAD_WIDTH // 2,), jnp.float32, math.log(1.0), math.log(32.0))), 1.0, 32.0)
    output_weight = scatter_about(arg_keys[7], (KEY_HEADS, QUERIES_PER_KEY * HEAD_WIDTH, MODEL_WIDTH), (QUERY_HEADS * HEAD_WIDTH) ** -0.5, 0.09375, ((0, 4), (1, 4), (2, 2)))
    return {"q_long": q_long, "long_key_value": long_key_value, "q_short": q_short, "short_key_value": short_key_value, "doc_ids": doc_ids, "live_counts": live_counts, "rescale": rescale, "output_weight": output_weight}


NEGATIVE_FILL = -1e+30
ROPE_BASE = 500000.0

def apply_head_rotation(value_tensor, positions, rescale):
    head_size = value_tensor.shape[-1]
    half_size = head_size // 2
    exponents = jnp.arange(half_size, dtype=jnp.float32) * (2.0 / head_size)
    inverse = jnp.exp(-exponents * math.log(ROPE_BASE)) / rescale
    angles = positions.astype(jnp.float32)[:, None] * inverse[None, :]
    cosine = jnp.cos(angles)[:, None, :]
    sine = jnp.sin(angles)[:, None, :]
    first_half = value_tensor[..., :half_size]
    second_half = value_tensor[..., half_size:]
    return jnp.concatenate([first_half * cosine - second_half * sine, second_half * cosine + first_half * sine], axis=-1)

def attend(query_rows, key_rows, value_rows, visible):
    scores = jnp.dot(query_rows, key_rows.T, preferred_element_type=jnp.float32) * (1.0 / math.sqrt(query_rows.shape[-1]))
    scores = jnp.where(visible, scores, NEGATIVE_FILL)
    row_max = lax.optimization_barrier(jnp.max(scores, axis=-1, keepdims=True))
    weights = jnp.where(visible, jnp.exp(scores - row_max), 0.0)
    summed = lax.optimization_barrier(jnp.sum(weights, axis=-1, keepdims=True))
    weighted = jnp.dot(weights.astype(jnp.bfloat16), value_rows, preferred_element_type=jnp.float32)
    return (weighted / summed).astype(jnp.bfloat16)

def reference(q_long, long_key_value, q_short, short_key_value, doc_ids, live_counts, rescale, output_weight):
    long_token_positions = jnp.arange(LONG_DOC_ROWS, dtype=jnp.int32)
    long_queries = jax.vmap(lambda value_tensor: apply_head_rotation(value_tensor, long_token_positions, rescale))(q_long.astype(jnp.float32).reshape(N_DP, LONG_DOC_ROWS, QUERY_HEADS, HEAD_WIDTH)).astype(jnp.bfloat16)
    long_key_rows = jax.vmap(lambda value_tensor: apply_head_rotation(value_tensor, long_token_positions, rescale))(long_key_value[:, 0].astype(jnp.float32).reshape(N_DP, LONG_DOC_ROWS, KEY_HEADS, HEAD_WIDTH)).astype(jnp.bfloat16)
    long_value_rows = long_key_value[:, 1].reshape(N_DP, LONG_DOC_ROWS, KEY_HEADS, HEAD_WIDTH)
    causal = long_token_positions[None, :] <= long_token_positions[:, None]
    query_items = long_queries.transpose(0, 2, 1, 3).reshape(N_DP * QUERY_HEADS, LONG_DOC_ROWS, HEAD_WIDTH)
    key_items = long_key_rows.transpose(0, 2, 1, 3)
    value_items = long_value_rows.transpose(0, 2, 1, 3)

    def long_item(item_id):
        group_id = item_id // QUERY_HEADS
        head_id = item_id % QUERY_HEADS
        return attend(query_items[item_id], key_items[group_id, head_id // QUERIES_PER_KEY], value_items[group_id, head_id // QUERIES_PER_KEY], causal)
    long_attn = lax.map(long_item, jnp.arange(N_DP * QUERY_HEADS, dtype=jnp.int32))
    long_attn = long_attn.reshape(N_DP, QUERY_HEADS, LONG_DOC_ROWS, HEAD_WIDTH).transpose(0, 2, 1, 3).reshape(N_DP, LONG_DOC_ROWS, QUERY_HEADS * HEAD_WIDTH)
    row_index = jnp.arange(SLAB_SLOTS, dtype=jnp.int32)
    changes = jnp.concatenate([jnp.ones((SLAB_COUNT, 1), dtype=bool), doc_ids[:, 1:] != doc_ids[:, :-1]], axis=1)
    first_rows = lax.cummax(jnp.where(changes, row_index[None, :], 0).astype(jnp.int32), axis=1)
    short_token_positions = (row_index[None, :] - first_rows).astype(jnp.int32)
    short_queries = jax.vmap(apply_head_rotation, in_axes=(0, 0, None))(q_short.astype(jnp.float32).reshape(SLAB_COUNT, SLAB_SLOTS, QUERY_HEADS, HEAD_WIDTH), short_token_positions, rescale).astype(jnp.bfloat16)
    short_key_rows = jax.vmap(apply_head_rotation, in_axes=(0, 0, None))(short_key_value[:, 0].astype(jnp.float32).reshape(SLAB_COUNT, SLAB_SLOTS, KEY_HEADS, HEAD_WIDTH), short_token_positions, rescale).astype(jnp.bfloat16)
    short_value_rows = short_key_value[:, 1].reshape(SLAB_COUNT, SLAB_SLOTS, KEY_HEADS, HEAD_WIDTH)
    visible_short = (doc_ids[:, None, :] == doc_ids[:, :, None]) & (row_index[None, None, :] <= row_index[None, :, None])

    def short_item(item_id):
        slab_id = item_id // QUERY_HEADS
        head_id = item_id % QUERY_HEADS
        return attend(short_queries[slab_id, :, head_id], short_key_rows[slab_id, :, head_id // QUERIES_PER_KEY], short_value_rows[slab_id, :, head_id // QUERIES_PER_KEY], visible_short[slab_id])
    short_attn = lax.map(short_item, jnp.arange(SLAB_COUNT * QUERY_HEADS, dtype=jnp.int32))
    short_attn = short_attn.reshape(SLAB_COUNT, QUERY_HEADS, SLAB_SLOTS, HEAD_WIDTH).transpose(0, 2, 1, 3).reshape(SLAB_COUNT, SLAB_SLOTS, QUERY_HEADS * HEAD_WIDTH)
    packed = jnp.concatenate([long_attn.reshape(N_DP, N_CTX, LONG_DEV, QUERY_HEADS * HEAD_WIDTH), short_attn.reshape(N_DP, N_CTX, SLAB_SLOTS, QUERY_HEADS * HEAD_WIDTH)], axis=2)
    live_rows = (LONG_DEV + live_counts.reshape(N_DP, N_CTX)).astype(jnp.int32)
    offsets = (jnp.cumsum(live_rows, axis=1).astype(jnp.int32) - live_rows).astype(jnp.int32)
    slot_index = jnp.arange(SLOT, dtype=jnp.int32)
    targets = offsets[:, :, None] + slot_index[None, None, :]
    targets = jnp.where(slot_index[None, None, :] < live_rows[:, :, None], targets, GROUP_TOK).astype(jnp.int32)
    group_index = jnp.broadcast_to(jnp.arange(N_DP, dtype=jnp.int32)[:, None, None], targets.shape)
    dense_rows = jnp.zeros((N_DP, GROUP_TOK + 1, QUERY_HEADS * HEAD_WIDTH), jnp.bfloat16).at[group_index, targets].set(packed)[:, :GROUP_TOK]
    outputs = []
    for group_id in range(N_DP):
        summed = jnp.zeros((GROUP_TOK, MODEL_WIDTH), jnp.float32)
        for head_cluster in range(KEY_HEADS):
            head_rows = dense_rows[group_id, :, head_cluster * QUERIES_PER_KEY * HEAD_WIDTH:(head_cluster + 1) * QUERIES_PER_KEY * HEAD_WIDTH]
            partial_rows = jnp.dot(head_rows, output_weight[head_cluster], preferred_element_type=jnp.float32).astype(jnp.bfloat16)
            partial_rows = lax.optimization_barrier(partial_rows)
            summed = summed + partial_rows.astype(jnp.float32)
        outputs.append(summed.astype(jnp.bfloat16))
    return jnp.stack(outputs)
```

```python
import functools
import math

import jax
import jax.numpy as jnp
from jax import lax
from jax.experimental import pallas as pl
from jax.experimental.pallas import tpu as pltpu
from jax.sharding import PartitionSpec as P

NEGATIVE_FILL = -1e30
ROPE_BASE = 500000.0
COUNT_ROWS = 8
VMEM_LIMIT = 56 * 1024 * 1024
OUT_TO_IN = [(0, 1), (3, 2)]
IN_TO_OUT = [(1, 0), (2, 3)]
INNER = [(1, 2), (2, 1)]

SMEM_SPEC = pl.BlockSpec(memory_space=pltpu.SMEM)


def params():
    return pltpu.CompilerParams(vmem_limit_bytes=VMEM_LIMIT)


def half_turn(x, half):
    return jnp.concatenate([x[:, half:], x[:, :half]], axis=1)


def prepare_kernel(place_ref, kv_ref, doc_ref, rescale_ref, cos_ref, sin_ref, pair_ref):
    long_rows, head = kv_ref.shape[1], kv_ref.shape[2]
    half = head // 2
    slots = doc_ref.shape[1]
    lane = lax.broadcasted_iota(jnp.int32, (1, head), 1)
    frequency = jnp.where(lane < half, lane, lane - half).astype(jnp.float32)
    inverse = jnp.exp(-(frequency * (2.0 / head)) * math.log(ROPE_BASE)) / rescale_ref[...]
    sign = jnp.where(lane < half, -1.0, 1.0)
    row = lax.broadcasted_iota(jnp.int32, (long_rows, 1), 0) + place_ref[0] * long_rows
    angles = row.astype(jnp.float32) * inverse
    cosine, sine = jnp.cos(angles), jnp.sin(angles) * sign
    cos_ref[:long_rows, :] = cosine
    sin_ref[:long_rows, :] = sine
    keys = kv_ref[0].astype(jnp.float32)
    pair_ref[0] = (keys * cosine + half_turn(keys, half) * sine).astype(jnp.bfloat16)
    pair_ref[1] = kv_ref[1]
    docs = jnp.broadcast_to(doc_ref[...].astype(jnp.float32), (slots, slots))
    before = jnp.where(docs < docs.T, 1.0, 0.0)
    first = jnp.sum(before, axis=1, keepdims=True)
    slot = lax.broadcasted_iota(jnp.int32, (slots, 1), 0).astype(jnp.float32)
    short_angles = (slot - first) * inverse
    cos_ref[long_rows:, :] = jnp.cos(short_angles)
    sin_ref[long_rows:, :] = jnp.sin(short_angles) * sign


def prepare(place, kv, doc, rescale):
    slots, rows, head = doc.shape[1], kv.shape[1], kv.shape[2]
    table = jax.ShapeDtypeStruct((rows + slots, head), jnp.float32)
    return pl.pallas_call(
        prepare_kernel,
        in_specs=[SMEM_SPEC] + [pl.BlockSpec(memory_space=pltpu.VMEM)] * 3,
        out_specs=[pl.BlockSpec(memory_space=pltpu.VMEM)] * 3,
        out_shape=[table, table, jax.ShapeDtypeStruct(kv.shape, jnp.bfloat16)],
        compiler_params=params(),
        name="prepare",
    )(place, kv, doc, rescale)


def weigh(scores, visible, values):
    scores = [jnp.where(v, s, NEGATIVE_FILL) for s, v in zip(scores, visible)]
    peak = functools.reduce(jnp.maximum, [jnp.max(s, axis=1, keepdims=True) for s in scores])
    total, weighted = 0.0, 0.0
    for s, v, value in zip(scores, visible, values):
        weights = jnp.where(v, jnp.exp(s - peak), 0.0)
        total = total + jnp.sum(weights, axis=1, keepdims=True)
        weighted = weighted + jnp.dot(
            weights.astype(jnp.bfloat16), value, preferred_element_type=jnp.float32
        )
    return (weighted / total).astype(jnp.bfloat16)


def dot_t(a, b):
    return lax.dot_general(a, b, (((1,), (1,)), ((), ())), preferred_element_type=jnp.float32)


def attend_kernel(n_blocks, base_ref, ql_ref, qs_ref, skv_ref, doc_ref, cos_ref, sin_ref, *rest):
    pairs, out_ref = rest[:n_blocks], rest[n_blocks]
    long_rows, slots = ql_ref.shape[0], qs_ref.shape[0]
    head = cos_ref.shape[1]
    half = head // 2
    scale = 1.0 / math.sqrt(head)
    heads = ql_ref.shape[1] // head
    cosine, sine = cos_ref[...], sin_ref[...]

    def turn(x, first, last):
        return (x * cosine[first:last] + half_turn(x, half) * sine[first:last]).astype(jnp.bfloat16)

    row = lax.broadcasted_iota(jnp.int32, (long_rows, 1), 0) + base_ref[0] * long_rows
    visible = [
        lax.broadcasted_iota(jnp.int32, (long_rows, p.shape[1]), 1) + base_ref[1 + i] <= row
        for i, p in enumerate(pairs)
    ]
    short_keys = turn(skv_ref[0].astype(jnp.float32), long_rows, long_rows + slots)
    docs = jnp.broadcast_to(doc_ref[...].astype(jnp.float32), (slots, slots))
    below = lax.broadcasted_iota(jnp.int32, (slots, slots), 1) <= lax.broadcasted_iota(
        jnp.int32, (slots, slots), 0
    )
    short_visible = [(docs == docs.T) & below]
    short_values = [skv_ref[1]]
    for h in range(heads):
        columns = slice(h * head, (h + 1) * head)
        query = turn(ql_ref[:, columns].astype(jnp.float32), 0, long_rows)
        scores = [dot_t(query, p[0]) * scale for p in pairs]
        out_ref[:long_rows, columns] = weigh(scores, visible, [p[1] for p in pairs])
        query = turn(qs_ref[:, columns].astype(jnp.float32), long_rows, long_rows + slots)
        scores = [dot_t(query, short_keys) * scale]
        out_ref[long_rows : long_rows + slots, columns] = weigh(scores, short_visible, short_values)
    live = jnp.full((COUNT_ROWS, out_ref.shape[1]), base_ref[1 + n_blocks], jnp.int32)
    out_ref[long_rows + slots :, :] = live.astype(jnp.float32).astype(jnp.bfloat16)


def attend(scalars, q_long, q_short, short_kv, doc, cosine, sine, pairs):
    rows = q_long.shape[0] + q_short.shape[0] + COUNT_ROWS
    vmem = pl.BlockSpec(memory_space=pltpu.VMEM)
    return pl.pallas_call(
        functools.partial(attend_kernel, len(pairs)),
        in_specs=[SMEM_SPEC] + [vmem] * (6 + len(pairs)),
        out_specs=vmem,
        out_shape=jax.ShapeDtypeStruct((rows, q_long.shape[1]), jnp.bfloat16),
        compiler_params=params(),
        name="attend",
    )(scalars, q_long, q_short, short_kv, doc, cosine, sine, *pairs)


def pack_kernel(long_rows, slots, group_rows, n_pieces, scalar_ref, *rest):
    pieces, (send_ref, keep_ref, dense) = rest[:-3], rest[-3:]
    piece_rows = long_rows + slots

    def live_of(piece, first):
        tail = piece[pl.ds(first + piece_rows, COUNT_ROWS), :]
        return jnp.max(tail.astype(jnp.float32)).astype(jnp.int32)

    def put(piece, first, offset):
        rows = piece[pl.ds(first, piece_rows), :].astype(jnp.float32)
        dense[pl.ds(pl.multiple_of(offset, 8), piece_rows), :] = rows
        return offset + long_rows + live_of(piece, first)

    if len(pieces) == 1:
        offset = jnp.int32(0)
        for i in range(n_pieces):
            offset = put(pieces[0], i * (piece_rows + COUNT_ROWS), offset)
    else:
        mine, theirs = pieces

        @pl.when(scalar_ref[0] == 0)
        def _():
            put(theirs, 0, put(mine, 0, jnp.int32(0)))

        @pl.when(scalar_ref[0] != 0)
        def _():
            put(mine, 0, put(theirs, 0, jnp.int32(0)))

    quarter = group_rows // 4
    for ref, first in ((send_ref, 1), (keep_ref, 3)):
        for s in range(2):
            start = pl.multiple_of(scalar_ref[first + s] * quarter, 8)
            ref[s * quarter : (s + 1) * quarter, :] = dense[pl.ds(start, quarter), :].astype(
                jnp.bfloat16
            )


def pack(scalars, pieces, long_rows, slots, n_pieces):
    group_rows = n_pieces * (long_rows + 3 * slots // 4)
    columns = pieces[0].shape[1]
    block = columns // 4
    out = jax.ShapeDtypeStruct((group_rows // 2, columns), jnp.bfloat16)
    out_spec = pl.BlockSpec((group_rows // 2, block), lambda j, s: (0, j))
    return pl.pallas_call(
        functools.partial(pack_kernel, long_rows, slots, group_rows, n_pieces),
        grid_spec=pltpu.PrefetchScalarGridSpec(
            num_scalar_prefetch=1,
            grid=(4,),
            in_specs=[pl.BlockSpec((p.shape[0], block), lambda j, s: (0, s[5 + j])) for p in pieces],
            out_specs=[out_spec, out_spec],
            scratch_shapes=[pltpu.VMEM((group_rows + long_rows + slots, block), jnp.float32)],
        ),
        out_shape=[out, out],
        compiler_params=params(),
        name="pack",
    )(scalars, *pieces)


def project_kernel(with_add, inner_ref, own_ref, other_ref, *rest):
    weights, rest = rest[:4], rest[4:]
    rows = own_ref.shape[0]
    depth = weights[0].shape[0]
    for part, a_ref in enumerate((own_ref, other_ref)):
        out_ref, here = (rest[-2 + part], slice(0, rows)) if with_add else (
            rest[-1],
            slice(part * rows, (part + 1) * rows),
        )

        @pl.when(inner_ref[0] != 0)
        def _(part=part, a_ref=a_ref, out_ref=out_ref, here=here):
            total = functools.reduce(
                jnp.add,
                [
                    jnp.dot(
                        a_ref[:, i * depth : (i + 1) * depth],
                        w[...],
                        preferred_element_type=jnp.float32,
                    )
                    for i, w in enumerate(weights)
                ],
            )
            if with_add:
                total = total + rest[0][part * rows : (part + 1) * rows, :].astype(jnp.float32)
            out_ref[here, :] = total.astype(jnp.bfloat16)

        @pl.when(inner_ref[0] == 0)
        def _(out_ref=out_ref, here=here):
            out_ref[here, :] = jnp.zeros((rows, out_ref.shape[1]), jnp.bfloat16)


def project(inner, own, other, weights, received=None):
    rows, width = own.shape
    depth, columns = weights[0].shape
    tile = 512 if columns % 512 == 0 else 128
    full = pl.BlockSpec((rows, width), lambda j: (0, 0), pipeline_mode=pl.Buffered(1))
    both = pl.BlockSpec((2 * rows, tile), lambda j: (0, j))
    one = pl.BlockSpec((rows, tile), lambda j: (0, j))
    in_specs = [SMEM_SPEC, full, full] + [pl.BlockSpec((depth, tile), lambda j: (0, j))] * 4
    args = [inner, own, other, *weights]
    if received is None:
        out_specs = both
        out_shape = jax.ShapeDtypeStruct((2 * rows, columns), jnp.bfloat16)
    else:
        in_specs.append(both)
        args.append(received)
        out_specs = [one, one]
        out_shape = [jax.ShapeDtypeStruct((rows, columns), jnp.bfloat16)] * 2
    return pl.pallas_call(
        functools.partial(project_kernel, received is not None),
        grid=(columns // tile,),
        in_specs=in_specs,
        out_specs=out_specs,
        out_shape=out_shape,
        compiler_params=params(),
        name="project",
    )(*args)


def column_chunks(columns):
    unit = columns // 8
    if unit % 512:
        return [columns]
    return [3 * unit, 3 * unit, 2 * unit]


def local(
    q_long, long_key_value, q_short, short_key_value, doc_ids, live_counts, rescale, output_weight
):
    head = rescale.shape[0] * 2
    long_rows, slots = q_long.shape[1], q_short.shape[1]
    ctx, tp, dp = lax.axis_index("ctx"), lax.axis_index("tp"), lax.axis_index("dp")
    n_ctx = lax.axis_size("ctx")
    is_inner = (dp == 1) | (dp == 2)

    def swap_ctx(x):
        return lax.ppermute(x, "ctx", [(0, 1), (1, 0)])

    weight = output_weight[0]
    chunks, weights = column_chunks(weight.shape[1]), []
    start = 0
    for width in chunks:
        own = lax.slice_in_dim(weight, start, start + width, axis=1)
        start += width
        twin = lax.ppermute(own, "dp", INNER)
        near = lax.ppermute(own, "dp", OUT_TO_IN)
        far = lax.ppermute(near, "dp", INNER)
        weights.append((own, twin, near, far))
    near_plane = jnp.where(dp < 2, 0, 3)
    blocks = [dp, 3 - dp, near_plane, 3 - near_plane]

    cosine, sine, pair = prepare(
        ctx.reshape(1).astype(jnp.int32),
        long_key_value[0],
        doc_ids,
        jnp.concatenate([rescale, rescale]).reshape(1, head),
    )
    if n_ctx == 2:
        pairs = [pair, swap_ctx(pair)]
        bases = [ctx * long_rows, (1 - ctx) * long_rows]
    else:
        pairs = [lax.all_gather(pair, "ctx", axis=1, tiled=True)]
        bases = [jnp.int32(0)]
    rows = attend(
        jnp.stack([ctx, *bases, live_counts[0]]).astype(jnp.int32),
        q_long[0],
        q_short[0],
        short_key_value[0],
        doc_ids,
        cosine,
        sine,
        pairs,
    )

    scalars = jnp.stack(
        [ctx, (tp ^ 2) ^ 1, tp ^ 1, tp ^ 2, tp, *blocks]
    ).astype(jnp.int32)

    def gathered(x):
        if n_ctx == 2:
            return [x, swap_ctx(x)]
        return [lax.all_gather(x, "ctx", axis=0, tiled=True)]

    own_send, own_keep = pack(scalars, gathered(rows), long_rows, slots, n_ctx)
    other_rows = lax.ppermute(rows, "dp", OUT_TO_IN)
    other_send, other_keep = pack(scalars, gathered(other_rows), long_rows, slots, n_ctx)

    inner = is_inner.reshape(1).astype(jnp.int32)
    quarter = own_send.shape[0] // 2
    outputs = []
    for w in weights:
        partial = project(inner, own_send, other_send, w)
        received = lax.ppermute(partial, "tp", [(i, i ^ 1) for i in range(4)])
        own, other = project(inner, own_keep, other_keep, w, received)
        returned = lax.ppermute(other, "dp", IN_TO_OUT)
        summed = jnp.where(is_inner, own, returned)
        crossed = lax.ppermute(summed[:quarter], "tp", [(i, i ^ 2) for i in range(4)])
        outputs.append(
            (summed[quarter:].astype(jnp.float32) + crossed.astype(jnp.float32)).astype(
                jnp.bfloat16
            )
        )
    return jnp.concatenate(outputs, axis=1)[None]


def solution(mesh):
    in_specs = (
        P("dp", "ctx", "tp"),
        P("dp", None, "ctx", "tp"),
        P(("dp", "ctx"), None, "tp"),
        P(("dp", "ctx"), None, None, "tp"),
        P(("dp", "ctx"), None),
        P(("dp", "ctx")),
        P(),
        P("tp", "dp", "ctx"),
    )
    out_specs = P("dp", "tp", "ctx")
    return jax.shard_map(local, mesh=mesh, in_specs=in_specs, out_specs=out_specs, check_vma=False)
```

```python
import functools
import math

import jax
import jax.numpy as jnp
from jax import lax
from jax.experimental import pallas as pl
from jax.experimental.pallas import tpu as pltpu
from jax.sharding import PartitionSpec as P

NEGATIVE_FILL = -1e30
ROPE_BASE = 500000.0
COUNT_ROWS = 8
FIRST_ROW, BASE, LIVE, CTX, HALVES, PLANE = 0, 1, 3, 4, 5, 7
VMEM_LIMIT = 56 * 1024 * 1024
SMALL_LIMIT = 12 * 1024 * 1024
OUT_TO_IN = [(0, 1), (3, 2)]
IN_TO_OUT = [(1, 0), (2, 3)]
INNER = [(1, 2), (2, 1)]
CORE = [(i, i ^ 1) for i in range(4)]
CROSS = [(i, i ^ 2) for i in range(4)]

SMEM_SPEC = pl.BlockSpec(memory_space=pltpu.SMEM)


def params(rows=0):
    limit = VMEM_LIMIT if rows > 512 else SMALL_LIMIT
    return pltpu.CompilerParams(vmem_limit_bytes=limit)


def send(x, axis, pairs, name):
    with jax.named_scope(name):
        return lax.ppermute(x, axis, pairs)


def after(value, *done):
    return lax.optimization_barrier((value, *done))[0]


def half_turn(x, half):
    return jnp.concatenate([x[:, half:], x[:, :half]], axis=1)


def prepare_kernel(n_blocks, base_ref, doc_ref, rescale_ref, *tables):
    slots = doc_ref.shape[1]
    head = rescale_ref.shape[1]
    half = head // 2
    lane = lax.broadcasted_iota(jnp.int32, (1, head), 1)
    frequency = jnp.where(lane < half, lane, lane - half).astype(jnp.float32)
    inverse = jnp.exp(-(frequency * (2.0 / head)) * math.log(ROPE_BASE)) / rescale_ref[...]
    sign = jnp.where(lane < half, -1.0, 1.0)
    docs = jnp.broadcast_to(doc_ref[...].astype(jnp.float32), (slots, slots))
    first = jnp.sum(jnp.where(docs < docs.T, 1.0, 0.0), axis=1, keepdims=True)
    slot = lax.broadcasted_iota(jnp.int32, (slots, 1), 0).astype(jnp.float32)
    for i in range(n_blocks + 1):
        cos_ref, sin_ref = tables[2 * i], tables[2 * i + 1]
        if i == n_blocks:
            position = slot - first
        else:
            rows = lax.broadcasted_iota(jnp.int32, (cos_ref.shape[0], 1), 0)
            position = (rows + base_ref[BASE + i]).astype(jnp.float32)
        angles = position * inverse
        cos_ref[...] = jnp.cos(angles)
        sin_ref[...] = jnp.sin(angles) * sign


def prepare(bases, block_rows, doc, rescale):
    vmem = pl.BlockSpec(memory_space=pltpu.VMEM)
    shapes = [
        jax.ShapeDtypeStruct((rows, rescale.shape[1]), jnp.float32)
        for rows in [*block_rows, doc.shape[1]]
        for _ in range(2)
    ]
    return pl.pallas_call(
        functools.partial(prepare_kernel, len(block_rows)),
        in_specs=[SMEM_SPEC, vmem, vmem],
        out_specs=[vmem] * len(shapes),
        out_shape=shapes,
        compiler_params=params(),
        name="prepare",
    )(bases, doc, rescale)


def weigh(scores, visible, values, scale):
    scores = [jnp.where(v, s, NEGATIVE_FILL) for s, v in zip(scores, visible)]
    peak = functools.reduce(jnp.maximum, [jnp.max(s, axis=1, keepdims=True) for s in scores])
    total, weighted = 0.0, 0.0
    for s, value in zip(scores, values):
        weights = jnp.exp2((s - peak) * (scale * math.log2(math.e)))
        total = total + jnp.sum(weights, axis=1, keepdims=True)
        weighted = weighted + jnp.dot(
            weights.astype(jnp.bfloat16), value, preferred_element_type=jnp.float32
        )
    return (weighted / total).astype(jnp.bfloat16)


def dot_t(a, b):
    return lax.dot_general(a, b, (((1,), (1,)), ((), ())), preferred_element_type=jnp.float32)


def turn(x, cosine, sine):
    x = x.astype(jnp.float32)
    return (x * cosine + half_turn(x, x.shape[1] // 2) * sine).astype(jnp.bfloat16)


def attend_kernel(n_blocks, n_tables, scalar_ref, ql_ref, qs_ref, skv_ref, doc_ref, *rest):
    tables, rest = rest[:n_tables], rest[n_tables:]
    pairs, rest = rest[:n_blocks], rest[n_blocks:]
    out_ref = rest[-1]
    long_rows, slots = ql_ref.shape[0], qs_ref.shape[0]
    head = skv_ref.shape[2]
    scale = 1.0 / math.sqrt(head)
    heads = ql_ref.shape[1] // head
    if n_tables == 2 * n_blocks + 2:
        own_table = (tables[0][...], tables[1][...])
    else:
        own_table = (tables[-4][...], tables[-3][...])
    slab_table = (tables[-2][...], tables[-1][...])
    keys = [turn(p[0], tables[2 * i][...], tables[2 * i + 1][...]) for i, p in enumerate(pairs)]
    values = [p[1] for p in pairs]
    row = lax.broadcasted_iota(jnp.int32, (long_rows, 1), 0) + scalar_ref[FIRST_ROW]
    visible = [
        lax.broadcasted_iota(jnp.int32, (long_rows, p.shape[1]), 1) + scalar_ref[BASE + i] <= row
        for i, p in enumerate(pairs)
    ]
    short_keys = turn(skv_ref[0], *slab_table)
    docs = jnp.broadcast_to(doc_ref[...].astype(jnp.float32), (slots, slots))
    below = lax.broadcasted_iota(jnp.int32, (slots, slots), 1) <= lax.broadcasted_iota(
        jnp.int32, (slots, slots), 0
    )
    short_visible = [(docs == docs.T) & below]
    short_values = [skv_ref[1]]
    for h in range(heads):
        columns = slice(h * head, (h + 1) * head)
        query = turn(ql_ref[:, columns], *own_table)
        scores = [dot_t(query, k) for k in keys]
        out_ref[:long_rows, columns] = weigh(scores, visible, values, scale)
        query = turn(qs_ref[:, columns], *slab_table)
        out_ref[long_rows : long_rows + slots, columns] = weigh(
            [dot_t(query, short_keys)], short_visible, short_values, scale
        )
    live = jnp.full((COUNT_ROWS, out_ref.shape[1]), scalar_ref[LIVE], jnp.int32)
    out_ref[long_rows + slots :, :] = live.astype(jnp.float32).astype(jnp.bfloat16)


def attend(scalars, q_long, q_short, short_kv, doc, tables, pairs):
    rows = q_long.shape[0] + q_short.shape[0] + COUNT_ROWS
    vmem = pl.BlockSpec(memory_space=pltpu.VMEM)
    return pl.pallas_call(
        functools.partial(attend_kernel, len(pairs), len(tables)),
        in_specs=[SMEM_SPEC] + [vmem] * (4 + len(tables) + len(pairs)),
        out_specs=vmem,
        out_shape=jax.ShapeDtypeStruct((rows, q_long.shape[1]), jnp.bfloat16),
        compiler_params=params(sum(p.shape[1] for p in pairs)),
        name="attend",
    )(scalars, q_long, q_short, short_kv, doc, *tables, *pairs)


def pack_kernel(long_rows, slots, group_rows, n_pieces, scalar_ref, *rest):
    pieces, (out_ref, dense) = rest[:-2], rest[-2:]
    piece_rows = long_rows + slots

    def live_of(piece, first):
        tail = piece[pl.ds(first + piece_rows, COUNT_ROWS), :]
        return jnp.max(tail.astype(jnp.float32)).astype(jnp.int32)

    def put(piece, first, offset):
        rows = piece[pl.ds(first, piece_rows), :].astype(jnp.float32)
        dense[pl.ds(pl.multiple_of(offset, 8), piece_rows), :] = rows
        return offset + long_rows + live_of(piece, first)

    if len(pieces) == 1:
        offset = jnp.int32(0)
        for i in range(n_pieces):
            offset = put(pieces[0], i * (piece_rows + COUNT_ROWS), offset)
    else:
        mine, theirs = pieces

        @pl.when(scalar_ref[CTX] == 0)
        def _():
            put(theirs, 0, put(mine, 0, jnp.int32(0)))

        @pl.when(scalar_ref[CTX] != 0)
        def _():
            put(mine, 0, put(theirs, 0, jnp.int32(0)))

    half = group_rows // 2
    for s in range(2):
        start = pl.multiple_of(scalar_ref[HALVES + s] * half, 8)
        out_ref[s * half : (s + 1) * half, :] = dense[pl.ds(start, half), :].astype(jnp.bfloat16)


def pack(place, pieces, long_rows, slots, n_pieces):
    group_rows = n_pieces * (long_rows + 3 * slots // 4)
    columns = pieces[0].shape[1]
    block = min(columns, 512 if n_pieces == 2 else 256)
    return pl.pallas_call(
        functools.partial(pack_kernel, long_rows, slots, group_rows, n_pieces),
        grid_spec=pltpu.PrefetchScalarGridSpec(
            num_scalar_prefetch=1,
            grid=(columns // block,),
            in_specs=[pl.BlockSpec((p.shape[0], block), lambda j, s: (0, j)) for p in pieces],
            out_specs=pl.BlockSpec((group_rows, block), lambda j, s: (0, j)),
            scratch_shapes=[pltpu.VMEM((group_rows + long_rows + slots, block), jnp.float32)],
        ),
        out_shape=jax.ShapeDtypeStruct((group_rows, columns), jnp.bfloat16),
        compiler_params=params(group_rows // 2),
        name="pack",
    )(place, *pieces)


def project_kernel(at, width, straight, plane_ref, *refs):
    rows, weights, outs = refs[:4], refs[4:8], refs[8:]
    depth = weights[0].shape[0] // 2
    half = rows[0].shape[0] // 2

    def block(i, part, a, b):
        here = slice(part * depth, (part + 1) * depth)
        return weights[i][here, a:b] if i == 3 else weights[i][here, at + a : at + b]

    for plane, order in ((1, (2, 0, 1, 3)), (2, (3, 1, 0, 2))):

        @pl.when(plane_ref[PLANE] == plane)
        def _(order=order):
            for first in range(0, width, 512):
                last = min(width, first + 512)
                for bounds in ((first, min(last, straight)), (max(first, straight), last)):
                    a, b = bounds
                    if a >= b:
                        continue
                    weight = jnp.concatenate(
                        [block(i, part, a, b) for part in range(2) for i in order], axis=0
                    )
                    for group in range(2):
                        left = jnp.concatenate([rows[2 * group][...], rows[2 * group + 1][...]], axis=1)
                        total = jnp.dot(left, weight, preferred_element_type=jnp.float32)
                        total = total.astype(jnp.bfloat16)
                        if b <= straight:
                            outs[group][:, a:b] = total
                        else:
                            here = slice(a - straight, b - straight)
                            there = slice(group * half, (group + 1) * half)
                            outs[-2][there, here] = total[:half]
                            outs[-1][there, here] = total[half:]

    @pl.when((plane_ref[PLANE] != 1) & (plane_ref[PLANE] != 2))
    def _():
        for out in outs:
            out[...] = jnp.zeros(out.shape, jnp.bfloat16)


def project(plane, rows, weights, at, width, straight):
    count = rows[0].shape[0]
    vmem = pl.BlockSpec(memory_space=pltpu.VMEM)
    shapes = [jax.ShapeDtypeStruct((count, w), jnp.bfloat16) for w in (straight, width - straight) if w for _ in range(2)]
    grid, row_spec, out_spec = (), vmem, vmem
    if count > 1024 and width == straight:
        block = count // 8
        grid = (8,)
        row_spec = pl.BlockSpec((block, rows[0].shape[1]), lambda i: (i, 0))
        out_spec = pl.BlockSpec((block, width), lambda i: (i, 0))
    return pl.pallas_call(
        functools.partial(project_kernel, at, width, straight),
        grid=grid,
        in_specs=[SMEM_SPEC] + [row_spec] * 4 + [vmem] * len(weights),
        out_specs=[out_spec] * len(shapes),
        out_shape=shapes,
        compiler_params=params(count // 2),
        name="project",
    )(plane, *rows, *weights)


def column_chunks(columns):
    unit = columns // 16
    if unit % 128:
        return [columns], [columns]
    return [7 * unit, 5 * unit, 4 * unit], [4 * unit, 2 * unit, 2 * unit]


def local(
    q_long, long_key_value, q_short, short_key_value, doc_ids, live_counts, rescale, output_weight
):
    head = rescale.shape[0] * 2
    long_rows, slots = q_long.shape[1], q_short.shape[1]
    ctx, tp, dp = lax.axis_index("ctx"), lax.axis_index("tp"), lax.axis_index("dp")
    n_ctx = lax.axis_size("ctx")
    own_base = ctx * long_rows
    bases = [own_base, (1 - ctx) * long_rows] if n_ctx == 2 else [jnp.int32(0), own_base]
    place = jnp.stack(
        [own_base, *bases, live_counts[0], ctx, 1 - (tp >> 1), tp >> 1, dp]
    ).astype(jnp.int32)
    weight = output_weight[0]
    width = weight.shape[1] // 2
    place, is_inner, is_left, keep_at, give_at, weight, doubled = lax.optimization_barrier(
        (
            place,
            (dp == 1) | (dp == 2),
            (tp & 1) == 0,
            (tp & 1) * width,
            (1 - (tp & 1)) * width,
            weight,
            jnp.concatenate([rescale, rescale]).reshape(1, head),
        )
    )

    def swap_ctx(x, name):
        return send(x, "ctx", [(0, 1), (1, 0)], name)

    widths, straight = column_chunks(width)
    n = len(widths)
    given = lax.dynamic_slice_in_dim(weight, give_at, width, 1)
    kept = lax.dynamic_slice_in_dim(weight, keep_at, width, 1)

    def trade(a, b, name):
        theirs = send(given[:, a:b], "tp", CORE, name)
        return jnp.concatenate([kept[:, a:b], theirs], axis=0)

    near, far = {}, {}
    both = [trade(0, widths[0], "trade0")]
    near[0] = send(both[0], "dp", OUT_TO_IN, "near0")
    twin = [send(both[0], "dp", INNER, "twin0")]
    if n > 1:
        both.append(trade(widths[0], width, "trade1"))

    def forward(i, source):
        far[i] = send(source, "dp", INNER, f"far{i}")

    raw = long_key_value[0]
    if n_ctx == 2:
        pairs = [raw, swap_ctx(raw, "keys")]
        block_rows = [long_rows, long_rows]
    else:
        pairs = [lax.all_gather(raw, "ctx", axis=1, tiled=True)]
        block_rows = [n_ctx * long_rows, long_rows]
    tables = prepare(place, block_rows, doc_ids, doubled)
    inputs = (place, q_long[0], q_short[0], short_key_value[0], doc_ids, tables, pairs)
    if n > 1:
        inputs = (after(place, both[1]), *inputs[1:])
    rows = attend(*inputs)
    forward(0, after(near[0], rows))
    rows = after(rows, near[0], twin[0])

    def gathered(x, name):
        if n_ctx == 2:
            return [x, swap_ctx(x, name)]
        return [lax.all_gather(x, "ctx", axis=0, tiled=True)]

    handed = send(rows, "dp", OUT_TO_IN, "hand")
    pieces = gathered(rows, "rows")
    other_pieces = gathered(handed, "other")
    if n > 1:
        rest = after(both[1], handed, far[0])
        twin.append(send(rest, "dp", INNER, "twin1"))
        near[1] = send(rest, "dp", OUT_TO_IN, "near1")
    pieces[-1] = after(pieces[-1], handed, far[0])
    own = pack(place, pieces, long_rows, slots, n_ctx)
    own_theirs = send(own, "tp", CORE, "own_rows")
    if n > 1:
        other_pieces[-1] = after(other_pieces[-1], near[1], own_theirs, twin[1])
        at = 0
        for i in range(1, n):
            forward(i, near[1][:, at : at + widths[i]])
            at += widths[i]
    other = pack(place, other_pieces, long_rows, slots, n_ctx)
    other_theirs = send(other, "tp", CORE, "other_rows")
    group = (own, own_theirs, other, other_theirs)

    def add(a, b):
        return (a.astype(jnp.float32) + b.astype(jnp.float32)).astype(jnp.bfloat16)

    def first_hop(i):
        part = min(i, 1)
        at = sum(widths[1:i])
        weights = (both[part], twin[part], near[part], far[i])
        outs = project(place, group, weights, at, widths[i], straight[i])
        hop = {}
        if straight[i]:
            hop["mine"], other_part = outs[0], outs[1]
            hop["returned"] = send(other_part, "dp", IN_TO_OUT, f"return{i}")
        if straight[i] < widths[i]:
            hop["kept"] = outs[-1]
            hop["crossed"] = send(outs[-2], "tp", CROSS, f"cross{i}")
        return hop, outs[0]

    def second_hop(i, hop, *gates):
        done = {}
        if "returned" in hop:
            summed = jnp.where(is_inner, hop["mine"], after(hop["returned"], *gates))
            done["kept"] = summed[half:]
            done["crossed"] = send(summed[:half], "tp", CROSS, f"cross_after{i}")
        if "crossed" in hop:
            summed = add(hop["kept"], after(hop["crossed"], *gates))
            done["mine"] = summed[:half]
            done["returned"] = send(summed[half:], "dp", IN_TO_OUT, f"return_after{i}")
        return done

    def finish(done):
        parts = []
        if "crossed" in done:
            parts.append(add(done["kept"], done["crossed"]))
        if "returned" in done:
            parts.append(jnp.where(is_inner, done["mine"], done["returned"]))
        return parts

    half = own.shape[0] // 2
    hops, seconds = [], []
    for i in range(n):
        if i:
            far[i] = after(far[i], gate)
        hop, gate = first_hop(i)
        hops.append(hop)
        if i:
            seconds.append(second_hop(i - 1, hops[i - 1], gate))
    gates = list(seconds[-1].values()) if seconds else []
    seconds.append(second_hop(n - 1, hops[-1], *gates))
    quarter = half // 2
    mine, theirs = [], []
    for i, done in enumerate(seconds):
        x = jnp.concatenate(finish(done), axis=1)
        mine.append(jnp.where(is_left, x[:quarter], x[quarter:]))
        theirs.append(
            send(jnp.where(is_left, x[quarter:], x[:quarter]), "tp", CORE, f"rest{i}")
        )
    mine, theirs = jnp.concatenate(mine, axis=1), jnp.concatenate(theirs, axis=1)
    left = jnp.where(is_left, mine, theirs)
    right = jnp.where(is_left, theirs, mine)
    return jnp.concatenate([left, right], axis=1)[None]


def solution(mesh):
    in_specs = (
        P("dp", "ctx", "tp"),
        P("dp", None, "ctx", "tp"),
        P(("dp", "ctx"), None, "tp"),
        P(("dp", "ctx"), None, None, "tp"),
        P(("dp", "ctx"), None),
        P(("dp", "ctx")),
        P(),
        P("tp", "dp", "ctx"),
    )
    out_specs = P("dp", "tp", "ctx")
    return jax.shard_map(local, mesh=mesh, in_specs=in_specs, out_specs=out_specs, check_vma=False)
```

```python
import functools
import math

import jax
import jax.numpy as jnp
from jax import lax
from jax.experimental import pallas as pl
from jax.experimental.pallas import tpu as pltpu
from jax.sharding import PartitionSpec as P

NEGATIVE_FILL = -1e30
ROPE_BASE = 500000.0
COUNT_ROWS = 8
DEEP = 2
FIRST_ROW, BASE, LIVE, CTX, HALVES, PLANE = 0, 1, 3, 4, 5, 7
VMEM_LIMIT = 56 * 1024 * 1024
SMALL_LIMIT = 12 * 1024 * 1024
OUT_TO_IN = [(0, 1), (3, 2)]
IN_TO_OUT = [(1, 0), (2, 3)]
INNER = [(1, 2), (2, 1)]
CORE = [(i, i ^ 1) for i in range(4)]
CROSS = [(i, i ^ 2) for i in range(4)]

SMEM_SPEC = pl.BlockSpec(memory_space=pltpu.SMEM)


def params(rows=0):
    limit = VMEM_LIMIT if rows > 512 else SMALL_LIMIT
    return pltpu.CompilerParams(vmem_limit_bytes=limit)


def send(x, axis, pairs, name):
    with jax.named_scope(name):
        return lax.ppermute(x, axis, pairs)


def after(value, *done):
    return lax.optimization_barrier((value, *done))[0]


def half_turn(x, half):
    return jnp.concatenate([x[:, half:], x[:, :half]], axis=1)


def prepare_kernel(n_blocks, base_ref, doc_ref, rescale_ref, *tables):
    slots = doc_ref.shape[1]
    head = rescale_ref.shape[1]
    half = head // 2
    lane = lax.broadcasted_iota(jnp.int32, (1, head), 1)
    frequency = jnp.where(lane < half, lane, lane - half).astype(jnp.float32)
    inverse = jnp.exp(-(frequency * (2.0 / head)) * math.log(ROPE_BASE)) / rescale_ref[...]
    sign = jnp.where(lane < half, -1.0, 1.0)
    docs = jnp.broadcast_to(doc_ref[...].astype(jnp.float32), (slots, slots))
    first = jnp.sum(jnp.where(docs < docs.T, 1.0, 0.0), axis=1, keepdims=True)
    slot = lax.broadcasted_iota(jnp.int32, (slots, 1), 0).astype(jnp.float32)
    for i in range(n_blocks + 1):
        cos_ref, sin_ref = tables[2 * i], tables[2 * i + 1]
        if i == n_blocks:
            position = slot - first
        else:
            rows = lax.broadcasted_iota(jnp.int32, (cos_ref.shape[0], 1), 0)
            position = (rows + base_ref[BASE + i]).astype(jnp.float32)
        angles = position * inverse
        cos_ref[...] = jnp.cos(angles)
        sin_ref[...] = jnp.sin(angles) * sign


def prepare(bases, block_rows, doc, rescale):
    vmem = pl.BlockSpec(memory_space=pltpu.VMEM)
    shapes = [
        jax.ShapeDtypeStruct((rows, rescale.shape[1]), jnp.float32)
        for rows in [*block_rows, doc.shape[1]]
        for _ in range(2)
    ]
    return pl.pallas_call(
        functools.partial(prepare_kernel, len(block_rows)),
        in_specs=[SMEM_SPEC, vmem, vmem],
        out_specs=[vmem] * len(shapes),
        out_shape=shapes,
        compiler_params=params(),
        name="prepare",
    )(bases, doc, rescale)


def weigh(scores, visible, values, scale):
    scores = [jnp.where(v, s, NEGATIVE_FILL) for s, v in zip(scores, visible)]
    peak = functools.reduce(jnp.maximum, [jnp.max(s, axis=1, keepdims=True) for s in scores])
    total, weighted = 0.0, 0.0
    for s, value in zip(scores, values):
        weights = jnp.exp2((s - peak) * (scale * math.log2(math.e)))
        total = total + jnp.sum(weights, axis=1, keepdims=True)
        weighted = weighted + jnp.dot(
            weights.astype(jnp.bfloat16), value, preferred_element_type=jnp.float32
        )
    return (weighted / total).astype(jnp.bfloat16)


def dot_t(a, b):
    return lax.dot_general(a, b, (((1,), (1,)), ((), ())), preferred_element_type=jnp.float32)


def turn(x, cosine, sine):
    x = x.astype(jnp.float32)
    return (x * cosine + half_turn(x, x.shape[1] // 2) * sine).astype(jnp.bfloat16)


def attend_kernel(n_blocks, n_tables, scalar_ref, ql_ref, qs_ref, skv_ref, doc_ref, *rest):
    tables, rest = rest[:n_tables], rest[n_tables:]
    pairs, rest = rest[:n_blocks], rest[n_blocks:]
    out_ref = rest[-1]
    long_rows, slots = ql_ref.shape[0], qs_ref.shape[0]
    head = skv_ref.shape[2]
    scale = 1.0 / math.sqrt(head)
    heads = ql_ref.shape[1] // head
    if n_tables == 2 * n_blocks + 2:
        own_table = (tables[0][...], tables[1][...])
    else:
        own_table = (tables[-4][...], tables[-3][...])
    slab_table = (tables[-2][...], tables[-1][...])
    keys = [turn(p[0], tables[2 * i][...], tables[2 * i + 1][...]) for i, p in enumerate(pairs)]
    values = [p[1] for p in pairs]
    row = lax.broadcasted_iota(jnp.int32, (long_rows, 1), 0) + scalar_ref[FIRST_ROW]
    visible = [
        lax.broadcasted_iota(jnp.int32, (long_rows, p.shape[1]), 1) + scalar_ref[BASE + i] <= row
        for i, p in enumerate(pairs)
    ]
    short_keys = turn(skv_ref[0], *slab_table)
    docs = jnp.broadcast_to(doc_ref[...].astype(jnp.float32), (slots, slots))
    below = lax.broadcasted_iota(jnp.int32, (slots, slots), 1) <= lax.broadcasted_iota(
        jnp.int32, (slots, slots), 0
    )
    short_visible = [(docs == docs.T) & below]
    short_values = [skv_ref[1]]
    for h in range(heads):
        columns = slice(h * head, (h + 1) * head)
        query = turn(ql_ref[:, columns], *own_table)
        scores = [dot_t(query, k) for k in keys]
        out_ref[:long_rows, columns] = weigh(scores, visible, values, scale)
        query = turn(qs_ref[:, columns], *slab_table)
        out_ref[long_rows : long_rows + slots, columns] = weigh(
            [dot_t(query, short_keys)], short_visible, short_values, scale
        )
    live = jnp.full((COUNT_ROWS, out_ref.shape[1]), scalar_ref[LIVE], jnp.int32)
    out_ref[long_rows + slots :, :] = live.astype(jnp.float32).astype(jnp.bfloat16)


def attend(scalars, q_long, q_short, short_kv, doc, tables, pairs):
    rows = q_long.shape[0] + q_short.shape[0] + COUNT_ROWS
    vmem = pl.BlockSpec(memory_space=pltpu.VMEM)
    return pl.pallas_call(
        functools.partial(attend_kernel, len(pairs), len(tables)),
        in_specs=[SMEM_SPEC] + [vmem] * (4 + len(tables) + len(pairs)),
        out_specs=vmem,
        out_shape=jax.ShapeDtypeStruct((rows, q_long.shape[1]), jnp.bfloat16),
        compiler_params=params(sum(p.shape[1] for p in pairs)),
        name="attend",
    )(scalars, q_long, q_short, short_kv, doc, *tables, *pairs)


def pack_kernel(long_rows, slots, group_rows, n_pieces, scalar_ref, *rest):
    pieces, (out_ref, dense) = rest[:-2], rest[-2:]
    piece_rows = long_rows + slots

    def live_of(piece, first):
        tail = piece[pl.ds(first + piece_rows, COUNT_ROWS), :]
        return jnp.max(tail.astype(jnp.float32)).astype(jnp.int32)

    def put(piece, first, offset):
        rows = piece[pl.ds(first, piece_rows), :].astype(jnp.float32)
        dense[pl.ds(pl.multiple_of(offset, 8), piece_rows), :] = rows
        return offset + long_rows + live_of(piece, first)

    if len(pieces) == 1:
        offset = jnp.int32(0)
        for i in range(n_pieces):
            offset = put(pieces[0], i * (piece_rows + COUNT_ROWS), offset)
    else:
        mine, theirs = pieces

        @pl.when(scalar_ref[CTX] == 0)
        def _():
            put(theirs, 0, put(mine, 0, jnp.int32(0)))

        @pl.when(scalar_ref[CTX] != 0)
        def _():
            put(mine, 0, put(theirs, 0, jnp.int32(0)))

    half = group_rows // 2
    for s in range(2):
        start = pl.multiple_of(scalar_ref[HALVES + s] * half, 8)
        out_ref[s * half : (s + 1) * half, :] = dense[pl.ds(start, half), :].astype(jnp.bfloat16)


def pack(place, pieces, long_rows, slots, n_pieces):
    group_rows = n_pieces * (long_rows + 3 * slots // 4)
    columns = pieces[0].shape[1]
    block = min(columns, 512 if n_pieces == 2 else 256)
    return pl.pallas_call(
        functools.partial(pack_kernel, long_rows, slots, group_rows, n_pieces),
        grid_spec=pltpu.PrefetchScalarGridSpec(
            num_scalar_prefetch=1,
            grid=(columns // block,),
            in_specs=[pl.BlockSpec((p.shape[0], block), lambda j, s: (0, j)) for p in pieces],
            out_specs=pl.BlockSpec((group_rows, block), lambda j, s: (0, j)),
            scratch_shapes=[pltpu.VMEM((group_rows + long_rows + slots, block), jnp.float32)],
        ),
        out_shape=jax.ShapeDtypeStruct((group_rows, columns), jnp.bfloat16),
        compiler_params=params(group_rows // 2),
        name="pack",
    )(place, *pieces)


def project_kernel(at, width, straight, plane_ref, *refs):
    pieces = 2 if straight < width else 1
    count = 2 * pieces + 2
    rows, weights, outs = refs[:4], refs[4 : 4 + count], refs[4 + count :]
    depth = weights[0].shape[0] // 2
    half = rows[0].shape[0] // 2

    def block(i, part, a, b):
        here = slice(part * depth, (part + 1) * depth)
        if i > 1:
            return weights[2 * pieces + i - 2][here, a:b]
        sides, first = [], 0
        for ref in weights[i * pieces : (i + 1) * pieces]:
            x, y = max(at + a, first), min(at + b, first + ref.shape[1])
            if x < y:
                sides.append(ref[here, x - first : y - first])
            first += ref.shape[1]
        return sides[0] if len(sides) == 1 else jnp.concatenate(sides, axis=1)

    for plane, order in ((1, (2, 0, 1, 3)), (2, (3, 1, 0, 2))):

        @pl.when(plane_ref[PLANE] == plane)
        def _(order=order):
            for first in range(0, width, 512):
                last = min(width, first + 512)
                for bounds in ((first, min(last, straight)), (max(first, straight), last)):
                    a, b = bounds
                    if a >= b:
                        continue
                    weight = jnp.concatenate(
                        [block(i, part, a, b) for part in range(2) for i in order], axis=0
                    )
                    for group in range(2):
                        left = jnp.concatenate([rows[2 * group][...], rows[2 * group + 1][...]], axis=1)
                        total = jnp.dot(left, weight, preferred_element_type=jnp.float32)
                        total = total.astype(jnp.bfloat16)
                        if b <= straight:
                            outs[group][:, a:b] = total
                        else:
                            here = slice(a - straight, b - straight)
                            there = slice(group * half, (group + 1) * half)
                            outs[-2][there, here] = total[:half]
                            outs[-1][there, here] = total[half:]

    @pl.when((plane_ref[PLANE] != 1) & (plane_ref[PLANE] != 2))
    def _():
        for out in outs:
            out[...] = jnp.zeros(out.shape, jnp.bfloat16)


def project(plane, rows, weights, at, width, straight):
    count = rows[0].shape[0]
    vmem = pl.BlockSpec(memory_space=pltpu.VMEM)
    shapes = [jax.ShapeDtypeStruct((count, w), jnp.bfloat16) for w in (straight, width - straight) if w for _ in range(2)]
    grid, row_spec, out_spec = (), vmem, vmem
    if count > 1024 and width == straight:
        block = count // 8
        grid = (8,)
        row_spec = pl.BlockSpec((block, rows[0].shape[1]), lambda i: (i, 0))
        out_spec = pl.BlockSpec((block, width), lambda i: (i, 0))
    return pl.pallas_call(
        functools.partial(project_kernel, at, width, straight),
        grid=grid,
        in_specs=[SMEM_SPEC] + [row_spec] * 4 + [vmem] * len(weights),
        out_specs=[out_spec] * len(shapes),
        out_shape=shapes,
        compiler_params=params(count // 2),
        name="project",
    )(plane, *rows, *weights)


def column_chunks(columns):
    unit = columns // 16
    if unit % 128:
        return [columns], [columns]
    return [4 * unit, 6 * unit, 6 * unit], [2 * unit, 3 * unit, 3 * unit]


def local(
    q_long, long_key_value, q_short, short_key_value, doc_ids, live_counts, rescale, output_weight
):
    head = rescale.shape[0] * 2
    long_rows, slots = q_long.shape[1], q_short.shape[1]
    ctx, tp, dp = lax.axis_index("ctx"), lax.axis_index("tp"), lax.axis_index("dp")
    n_ctx = lax.axis_size("ctx")
    own_base = ctx * long_rows
    bases = [own_base, (1 - ctx) * long_rows] if n_ctx == 2 else [jnp.int32(0), own_base]
    place = jnp.stack(
        [own_base, *bases, live_counts[0], ctx, 1 - (tp >> 1), tp >> 1, dp]
    ).astype(jnp.int32)
    weight = output_weight[0]
    width = weight.shape[1] // 2
    place, is_inner, is_left, keep_at, give_at, weight, doubled = lax.optimization_barrier(
        (
            place,
            (dp == 1) | (dp == 2),
            (tp & 1) == 0,
            (tp & 1) * width,
            (1 - (tp & 1)) * width,
            weight,
            jnp.concatenate([rescale, rescale]).reshape(1, head),
        )
    )

    def swap_ctx(x, name):
        return send(x, "ctx", [(0, 1), (1, 0)], name)

    widths, straight = column_chunks(width)
    n = len(widths)
    given = lax.dynamic_slice_in_dim(weight, give_at, width, 1)
    kept = lax.dynamic_slice_in_dim(weight, keep_at, width, 1)

    def trade(a, b, name):
        theirs = send(given[:, a:b], "tp", CORE, name)
        return jnp.concatenate([kept[:, a:b], theirs], axis=0)

    near, far = {}, {}
    cut = width // 2 if n > 1 else width
    both = [trade(0, cut, "trade0")]
    columns = [sum(widths[:i]) for i in range(n)]

    def fetch_near(i, *gates):
        if i < n:
            a, b = columns[i], columns[i] + widths[i]
            sides = []
            if a < cut:
                sides.append(both[0][:, a : min(b, cut)])
            if b > cut:
                sides.append(both[1][:, max(a, cut) - cut : b - cut])
            source = sides[0] if len(sides) == 1 else jnp.concatenate(sides, axis=1)
            near[i] = send(after(source, *gates), "dp", OUT_TO_IN, f"near{i}")

    fetch_near(0, place)
    twin = [send(both[0], "dp", INNER, "twin0")]
    if n > 1:
        both.append(trade(cut, width, "trade1"))

    def forward(i, *gates):
        if i < n:
            far[i] = send(after(near[i], *gates), "dp", INNER, f"far{i}")

    raw = long_key_value[0]
    if n_ctx == 2:
        pairs = [raw, swap_ctx(raw, "keys")]
        block_rows = [long_rows, long_rows]
    else:
        pairs = [lax.all_gather(raw, "ctx", axis=1, tiled=True)]
        block_rows = [n_ctx * long_rows, long_rows]
    tables = prepare(place, block_rows, doc_ids, doubled)
    inputs = (place, q_long[0], q_short[0], short_key_value[0], doc_ids, tables, pairs)
    if n > 1:
        inputs = (after(place, both[1]), *inputs[1:])
    rows = attend(*inputs)
    forward(0, rows)
    rows = after(rows, near[0])

    def gathered(x, name):
        if n_ctx == 2:
            return [x, swap_ctx(x, name)]
        return [lax.all_gather(x, "ctx", axis=0, tiled=True)]

    handed = send(rows, "dp", OUT_TO_IN, "hand")
    pieces = gathered(rows, "rows")
    other_pieces = gathered(handed, "other")
    if n > 1:
        twin.append(send(after(both[1], handed, twin[0]), "dp", INNER, "twin1"))
    fetch_near(1, handed, twin[0])
    pieces[-1] = after(pieces[-1], handed, far[0], twin[0])
    own = pack(place, pieces, long_rows, slots, n_ctx)
    own_theirs = send(own, "tp", CORE, "own_rows")
    if n > 1:
        other_pieces[-1] = after(other_pieces[-1], near[1], own_theirs, twin[1])
    other = pack(place, other_pieces, long_rows, slots, n_ctx)
    other_theirs = send(other, "tp", CORE, "other_rows")
    forward(1, other)
    fetch_near(2, other)
    group = (own, own_theirs, other, other_theirs)

    def add(a, b):
        return (a.astype(jnp.float32) + b.astype(jnp.float32)).astype(jnp.bfloat16)

    def first_hop(i):
        outs = project(
            place, group, (*both, *twin, near[i], far[i]), columns[i], widths[i], straight[i]
        )
        hop = {}
        if straight[i]:
            hop["mine"], other_part = outs[0], outs[1]
            hop["returned"] = send(other_part, "dp", IN_TO_OUT, f"return{i}")
        if straight[i] < widths[i]:
            hop["kept"] = outs[-1]
            hop["crossed"] = send(outs[-2], "tp", CROSS, f"cross{i}")
        return hop, outs[0]

    def second_hop(i, hop, *gates):
        done = {}
        if "returned" in hop:
            summed = jnp.where(is_inner, hop["mine"], after(hop["returned"], *gates))
            done["kept"] = summed[half:]
            done["crossed"] = send(summed[:half], "tp", CROSS, f"cross_after{i}")
        if "crossed" in hop:
            summed = add(hop["kept"], after(hop["crossed"], *gates))
            done["mine"] = summed[:half]
            done["returned"] = send(summed[half:], "dp", IN_TO_OUT, f"return_after{i}")
        return done

    def finish(done):
        parts = []
        if "crossed" in done:
            parts.append(add(done["kept"], done["crossed"]))
        if "returned" in done:
            parts.append(jnp.where(is_inner, done["mine"], done["returned"]))
        return parts

    half = own.shape[0] // 2
    hops, seconds = [], []
    for i in range(n):
        if i:
            gates = list(seconds[-1].values()) if i > 1 and i < DEEP else []
            seconds.append(second_hop(i - 1, hops[i - 1], *gates)) if i < DEEP else None
            leaving = [seconds[-1][k] for k in ("kept", "mine") if k in seconds[-1]]
            later = [near[i + 1]] if i + 1 < n else []
            far[i] = after(far[i], *leaving, *later)
            forward(i + 1)
        hop, gate = first_hop(i)
        hops.append(hop)
    for i in range(len(seconds), n):
        gates = list(seconds[-1].values()) if i else []
        seconds.append(second_hop(i, hops[i], gate, *gates))
    quarter = half // 2
    mine, theirs = [], []
    for i, done in enumerate(seconds):
        x = jnp.concatenate(finish(done), axis=1)
        mine.append(jnp.where(is_left, x[:quarter], x[quarter:]))
        theirs.append(
            send(jnp.where(is_left, x[quarter:], x[:quarter]), "tp", CORE, f"rest{i}")
        )
    mine, theirs = jnp.concatenate(mine, axis=1), jnp.concatenate(theirs, axis=1)
    left = jnp.where(is_left, mine, theirs)
    right = jnp.where(is_left, theirs, mine)
    return jnp.concatenate([left, right], axis=1)[None]


def solution(mesh):
    in_specs = (
        P("dp", "ctx", "tp"),
        P("dp", None, "ctx", "tp"),
        P(("dp", "ctx"), None, "tp"),
        P(("dp", "ctx"), None, None, "tp"),
        P(("dp", "ctx"), None),
        P(("dp", "ctx")),
        P(),
        P("tp", "dp", "ctx"),
    )
    out_specs = P("dp", "tp", "ctx")
    return jax.shard_map(local, mesh=mesh, in_specs=in_specs, out_specs=out_specs, check_vma=False)
```

```python
import functools
import math

import jax
import jax.numpy as jnp
from jax import lax
from jax.experimental import pallas as pl
from jax.experimental.pallas import tpu as pltpu
from jax.sharding import PartitionSpec as P

NEGATIVE_FILL = -1e30
ROPE_BASE = 500000.0
COUNT_ROWS = 8
DEEP = 2
FIRST_ROW, BASE, LIVE, CTX, HALVES, PLANE = 0, 1, 3, 4, 5, 7
VMEM_LIMIT = 56 * 1024 * 1024
SMALL_LIMIT = 12 * 1024 * 1024
OUT_TO_IN = [(0, 1), (3, 2)]
IN_TO_OUT = [(1, 0), (2, 3)]
INNER = [(1, 2), (2, 1)]
CORE = [(i, i ^ 1) for i in range(4)]
CROSS = [(i, i ^ 2) for i in range(4)]

SMEM_SPEC = pl.BlockSpec(memory_space=pltpu.SMEM)


def params(rows=0):
    limit = VMEM_LIMIT if rows > 512 else SMALL_LIMIT
    return pltpu.CompilerParams(vmem_limit_bytes=limit)


def send(x, axis, pairs, name):
    with jax.named_scope(name):
        return lax.ppermute(x, axis, pairs)


def after(value, *done):
    return lax.optimization_barrier((value, *done))[0]


def half_turn(x, half):
    return jnp.concatenate([x[:, half:], x[:, :half]], axis=1)


def prepare_kernel(n_blocks, base_ref, doc_ref, rescale_ref, *tables):
    slots = doc_ref.shape[1]
    half = rescale_ref.shape[1]
    head = 2 * half
    rescale = jnp.concatenate([rescale_ref[...], rescale_ref[...]], axis=1)
    lane = lax.broadcasted_iota(jnp.int32, (1, head), 1)
    frequency = jnp.where(lane < half, lane, lane - half).astype(jnp.float32)
    inverse = jnp.exp(-(frequency * (2.0 / head)) * math.log(ROPE_BASE)) / rescale
    sign = jnp.where(lane < half, -1.0, 1.0)
    docs = jnp.broadcast_to(doc_ref[...].astype(jnp.float32), (slots, slots))
    first = jnp.sum(jnp.where(docs < docs.T, 1.0, 0.0), axis=1, keepdims=True)
    slot = lax.broadcasted_iota(jnp.int32, (slots, 1), 0).astype(jnp.float32)
    for i in range(n_blocks + 1):
        cos_ref, sin_ref = tables[2 * i], tables[2 * i + 1]
        if i == n_blocks:
            position = slot - first
        else:
            rows = lax.broadcasted_iota(jnp.int32, (cos_ref.shape[0], 1), 0)
            position = (rows + base_ref[BASE + i]).astype(jnp.float32)
        angles = position * inverse
        cos_ref[...] = jnp.cos(angles)
        sin_ref[...] = jnp.sin(angles) * sign


def prepare(bases, block_rows, doc, rescale):
    vmem = pl.BlockSpec(memory_space=pltpu.VMEM)
    shapes = [
        jax.ShapeDtypeStruct((rows, 2 * rescale.shape[1]), jnp.float32)
        for rows in [*block_rows, doc.shape[1]]
        for _ in range(2)
    ]
    return pl.pallas_call(
        functools.partial(prepare_kernel, len(block_rows)),
        in_specs=[SMEM_SPEC, vmem, vmem],
        out_specs=[vmem] * len(shapes),
        out_shape=shapes,
        compiler_params=params(),
        name="prepare",
    )(bases, doc, rescale)


def weigh(scores, visible, values, scale):
    scores = [jnp.where(v, s, NEGATIVE_FILL) for s, v in zip(scores, visible)]
    peak = functools.reduce(jnp.maximum, [jnp.max(s, axis=1, keepdims=True) for s in scores])
    total, weighted = 0.0, 0.0
    for s, value in zip(scores, values):
        weights = jnp.exp2((s - peak) * (scale * math.log2(math.e)))
        total = total + jnp.sum(weights, axis=1, keepdims=True)
        weighted = weighted + jnp.dot(
            weights.astype(jnp.bfloat16), value, preferred_element_type=jnp.float32
        )
    return (weighted / total).astype(jnp.bfloat16)


def dot_t(a, b):
    return lax.dot_general(a, b, (((1,), (1,)), ((), ())), preferred_element_type=jnp.float32)


def turn(x, cosine, sine):
    x = x.astype(jnp.float32)
    return (x * cosine + half_turn(x, x.shape[1] // 2) * sine).astype(jnp.bfloat16)


def attend_kernel(n_blocks, n_tables, scalar_ref, ql_ref, qs_ref, skv_ref, doc_ref, *rest):
    tables, rest = rest[:n_tables], rest[n_tables:]
    pairs, rest = rest[:n_blocks], rest[n_blocks:]
    out_ref = rest[-1]
    long_rows, slots = ql_ref.shape[0], qs_ref.shape[0]
    head = skv_ref.shape[2]
    scale = 1.0 / math.sqrt(head)
    heads = ql_ref.shape[1] // head
    if n_tables == 2 * n_blocks + 2:
        own_table = (tables[0][...], tables[1][...])
    else:
        own_table = (tables[-4][...], tables[-3][...])
    slab_table = (tables[-2][...], tables[-1][...])
    keys = [turn(p[0], tables[2 * i][...], tables[2 * i + 1][...]) for i, p in enumerate(pairs)]
    values = [p[1] for p in pairs]
    row = lax.broadcasted_iota(jnp.int32, (long_rows, 1), 0) + scalar_ref[FIRST_ROW]
    visible = [
        lax.broadcasted_iota(jnp.int32, (long_rows, p.shape[1]), 1) + scalar_ref[BASE + i] <= row
        for i, p in enumerate(pairs)
    ]
    short_keys = turn(skv_ref[0], *slab_table)
    docs = jnp.broadcast_to(doc_ref[...].astype(jnp.float32), (slots, slots))
    below = lax.broadcasted_iota(jnp.int32, (slots, slots), 1) <= lax.broadcasted_iota(
        jnp.int32, (slots, slots), 0
    )
    short_visible = [(docs == docs.T) & below]
    short_values = [skv_ref[1]]
    for h in range(heads):
        columns = slice(h * head, (h + 1) * head)
        query = turn(ql_ref[:, columns], *own_table)
        scores = [dot_t(query, k) for k in keys]
        out_ref[:long_rows, columns] = weigh(scores, visible, values, scale)
        query = turn(qs_ref[:, columns], *slab_table)
        out_ref[long_rows : long_rows + slots, columns] = weigh(
            [dot_t(query, short_keys)], short_visible, short_values, scale
        )
    live = jnp.full((COUNT_ROWS, out_ref.shape[1]), scalar_ref[LIVE], jnp.int32)
    out_ref[long_rows + slots :, :] = live.astype(jnp.float32).astype(jnp.bfloat16)


def attend(scalars, q_long, q_short, short_kv, doc, tables, pairs):
    rows = q_long.shape[0] + q_short.shape[0] + COUNT_ROWS
    vmem = pl.BlockSpec(memory_space=pltpu.VMEM)
    return pl.pallas_call(
        functools.partial(attend_kernel, len(pairs), len(tables)),
        in_specs=[SMEM_SPEC] + [vmem] * (4 + len(tables) + len(pairs)),
        out_specs=vmem,
        out_shape=jax.ShapeDtypeStruct((rows, q_long.shape[1]), jnp.bfloat16),
        compiler_params=params(sum(p.shape[1] for p in pairs)),
        name="attend",
    )(scalars, q_long, q_short, short_kv, doc, *tables, *pairs)


def pack_kernel(long_rows, slots, group_rows, n_pieces, scalar_ref, *rest):
    pieces, (out_ref, dense) = rest[:-2], rest[-2:]
    piece_rows = long_rows + slots

    def live_of(piece, first):
        tail = piece[pl.ds(first + piece_rows, COUNT_ROWS), :]
        return jnp.max(tail.astype(jnp.float32)).astype(jnp.int32)

    def put(piece, first, offset):
        rows = piece[pl.ds(first, piece_rows), :].astype(jnp.float32)
        dense[pl.ds(pl.multiple_of(offset, 8), piece_rows), :] = rows
        return offset + long_rows + live_of(piece, first)

    if len(pieces) == 1:
        offset = jnp.int32(0)
        for i in range(n_pieces):
            offset = put(pieces[0], i * (piece_rows + COUNT_ROWS), offset)
    else:
        mine, theirs = pieces

        @pl.when(scalar_ref[CTX] == 0)
        def _():
            put(theirs, 0, put(mine, 0, jnp.int32(0)))

        @pl.when(scalar_ref[CTX] != 0)
        def _():
            put(mine, 0, put(theirs, 0, jnp.int32(0)))

    half = group_rows // 2
    for s in range(2):
        start = pl.multiple_of(scalar_ref[HALVES + s] * half, 8)
        out_ref[s * half : (s + 1) * half, :] = dense[pl.ds(start, half), :].astype(jnp.bfloat16)


def pack(place, pieces, long_rows, slots, n_pieces):
    group_rows = n_pieces * (long_rows + 3 * slots // 4)
    columns = pieces[0].shape[1]
    block = min(columns, 512 if n_pieces == 2 else 256)
    return pl.pallas_call(
        functools.partial(pack_kernel, long_rows, slots, group_rows, n_pieces),
        grid_spec=pltpu.PrefetchScalarGridSpec(
            num_scalar_prefetch=1,
            grid=(columns // block,),
            in_specs=[pl.BlockSpec((p.shape[0], block), lambda j, s: (0, j)) for p in pieces],
            out_specs=pl.BlockSpec((group_rows, block), lambda j, s: (0, j)),
            scratch_shapes=[pltpu.VMEM((group_rows + long_rows + slots, block), jnp.float32)],
        ),
        out_shape=jax.ShapeDtypeStruct((group_rows, columns), jnp.bfloat16),
        compiler_params=params(group_rows // 2),
        name="pack",
    )(place, *pieces)


def project_kernel(at, width, straight, plane_ref, *refs):
    pieces = 2 if straight < width else 1
    count = 2 * pieces + 2
    rows, weights, outs = refs[:4], refs[4 : 4 + count], refs[4 + count :]
    depth = weights[0].shape[0] // 2
    half = rows[0].shape[0] // 2

    def block(i, part, a, b):
        here = slice(part * depth, (part + 1) * depth)
        if i > 1:
            return weights[2 * pieces + i - 2][here, a:b]
        sides, first = [], 0
        for ref in weights[i * pieces : (i + 1) * pieces]:
            x, y = max(at + a, first), min(at + b, first + ref.shape[1])
            if x < y:
                sides.append(ref[here, x - first : y - first])
            first += ref.shape[1]
        return sides[0] if len(sides) == 1 else jnp.concatenate(sides, axis=1)

    for plane, order in ((1, (2, 0, 1, 3)), (2, (3, 1, 0, 2))):

        @pl.when(plane_ref[PLANE] == plane)
        def _(order=order):
            for first in range(0, width, 512):
                last = min(width, first + 512)
                for bounds in ((first, min(last, straight)), (max(first, straight), last)):
                    a, b = bounds
                    if a >= b:
                        continue
                    weight = jnp.concatenate(
                        [block(i, part, a, b) for part in range(2) for i in order], axis=0
                    )
                    for group in range(2):
                        left = jnp.concatenate([rows[2 * group][...], rows[2 * group + 1][...]], axis=1)
                        total = jnp.dot(left, weight, preferred_element_type=jnp.float32)
                        total = total.astype(jnp.bfloat16)
                        if b <= straight:
                            outs[group][:, a:b] = total
                        else:
                            here = slice(a - straight, b - straight)
                            there = slice(group * half, (group + 1) * half)
                            outs[-2][there, here] = total[:half]
                            outs[-1][there, here] = total[half:]

    @pl.when((plane_ref[PLANE] != 1) & (plane_ref[PLANE] != 2))
    def _():
        for out in outs:
            out[...] = jnp.zeros(out.shape, jnp.bfloat16)


def project(plane, rows, weights, at, width, straight):
    count = rows[0].shape[0]
    vmem = pl.BlockSpec(memory_space=pltpu.VMEM)
    shapes = [jax.ShapeDtypeStruct((count, w), jnp.bfloat16) for w in (straight, width - straight) if w for _ in range(2)]
    grid, row_spec, out_spec = (), vmem, vmem
    if count > 1024 and width == straight:
        block = count // 8
        grid = (8,)
        row_spec = pl.BlockSpec((block, rows[0].shape[1]), lambda i: (i, 0))
        out_spec = pl.BlockSpec((block, width), lambda i: (i, 0))
    return pl.pallas_call(
        functools.partial(project_kernel, at, width, straight),
        grid=grid,
        in_specs=[SMEM_SPEC] + [row_spec] * 4 + [vmem] * len(weights),
        out_specs=[out_spec] * len(shapes),
        out_shape=shapes,
        compiler_params=params(count // 2),
        name="project",
    )(plane, *rows, *weights)


def column_chunks(columns):
    unit = columns // 16
    if unit % 128:
        return [columns], [columns]
    return [4 * unit, 6 * unit, 6 * unit], [2 * unit, 3 * unit, 3 * unit]


def local(
    q_long, long_key_value, q_short, short_key_value, doc_ids, live_counts, rescale, output_weight
):
    head = rescale.shape[0] * 2
    long_rows, slots = q_long.shape[1], q_short.shape[1]
    ctx, tp, dp = lax.axis_index("ctx"), lax.axis_index("tp"), lax.axis_index("dp")
    n_ctx = lax.axis_size("ctx")
    own_base = ctx * long_rows
    bases = [own_base, (1 - ctx) * long_rows] if n_ctx == 2 else [jnp.int32(0), own_base]
    place = jnp.stack(
        [own_base, *bases, live_counts[0], ctx, 1 - (tp >> 1), tp >> 1, dp]
    ).astype(jnp.int32)
    weight = output_weight[0]
    width = weight.shape[1] // 2
    place, is_inner, is_left, keep_at, give_at, weight, factors = lax.optimization_barrier(
        (
            place,
            (dp == 1) | (dp == 2),
            (tp & 1) == 0,
            (tp & 1) * width,
            (1 - (tp & 1)) * width,
            weight,
            rescale.reshape(1, head // 2),
        )
    )

    def swap_ctx(x, name):
        return send(x, "ctx", [(0, 1), (1, 0)], name)

    widths, straight = column_chunks(width)
    n = len(widths)
    given = lax.dynamic_slice_in_dim(weight, give_at, width, 1)
    kept = lax.dynamic_slice_in_dim(weight, keep_at, width, 1)

    def trade(a, b, name):
        theirs = send(given[:, a:b], "tp", CORE, name)
        return jnp.concatenate([kept[:, a:b], theirs], axis=0)

    near, far = {}, {}
    cut = width // 2 if n > 1 else width
    both = [trade(0, cut, "trade0")]
    columns = [sum(widths[:i]) for i in range(n)]

    def fetch_near(i, *gates):
        if i < n:
            a, b = columns[i], columns[i] + widths[i]
            sides = []
            if a < cut:
                sides.append(both[0][:, a : min(b, cut)])
            if b > cut:
                sides.append(both[1][:, max(a, cut) - cut : b - cut])
            source = sides[0] if len(sides) == 1 else jnp.concatenate(sides, axis=1)
            near[i] = send(after(source, *gates), "dp", OUT_TO_IN, f"near{i}")

    fetch_near(0, place)
    twin = [send(both[0], "dp", INNER, "twin0")]
    if n > 1:
        both.append(trade(cut, width, "trade1"))

    def forward(i, *gates):
        if i < n:
            far[i] = send(after(near[i], *gates), "dp", INNER, f"far{i}")

    raw = long_key_value[0]
    if n_ctx == 2:
        pairs = [raw, swap_ctx(raw, "keys")]
        block_rows = [long_rows, long_rows]
    else:
        pairs = [lax.all_gather(raw, "ctx", axis=1, tiled=True)]
        block_rows = [n_ctx * long_rows, long_rows]
    tables = prepare(place, block_rows, doc_ids, factors)
    inputs = (place, q_long[0], q_short[0], short_key_value[0], doc_ids, tables, pairs)
    if n > 1:
        inputs = (after(place, both[1]), *inputs[1:])
    rows = attend(*inputs)
    forward(0, rows)
    rows = after(rows, near[0])

    def gathered(x, name):
        if n_ctx == 2:
            return [x, swap_ctx(x, name)]
        return [lax.all_gather(x, "ctx", axis=0, tiled=True)]

    handed = send(rows, "dp", OUT_TO_IN, "hand")
    pieces = gathered(rows, "rows")
    other_pieces = gathered(handed, "other")
    if n > 1:
        twin.append(send(after(both[1], handed, twin[0]), "dp", INNER, "twin1"))
    fetch_near(1, handed, twin[0])
    pieces[-1] = after(pieces[-1], handed, far[0], twin[0])
    own = pack(place, pieces, long_rows, slots, n_ctx)
    own_theirs = send(own, "tp", CORE, "own_rows")
    if n > 1:
        other_pieces[-1] = after(other_pieces[-1], near[1], own_theirs, twin[1])
    other = pack(place, other_pieces, long_rows, slots, n_ctx)
    other_theirs = send(other, "tp", CORE, "other_rows")
    forward(1, other)
    fetch_near(2, other)
    group = (own, own_theirs, other, other_theirs)

    def add(a, b):
        return (a.astype(jnp.float32) + b.astype(jnp.float32)).astype(jnp.bfloat16)

    def first_hop(i):
        outs = project(
            place, group, (*both, *twin, near[i], far[i]), columns[i], widths[i], straight[i]
        )
        hop = {}
        if straight[i]:
            hop["mine"], other_part = outs[0], outs[1]
            hop["returned"] = send(other_part, "dp", IN_TO_OUT, f"return{i}")
        if straight[i] < widths[i]:
            hop["kept"] = outs[-1]
            hop["crossed"] = send(outs[-2], "tp", CROSS, f"cross{i}")
        return hop, outs[0]

    def second_hop(i, hop, *gates):
        done = {}
        if "returned" in hop:
            summed = jnp.where(is_inner, hop["mine"], after(hop["returned"], *gates))
            done["kept"] = summed[half:]
            done["crossed"] = send(summed[:half], "tp", CROSS, f"cross_after{i}")
        if "crossed" in hop:
            summed = add(hop["kept"], after(hop["crossed"], *gates))
            done["mine"] = summed[:half]
            done["returned"] = send(summed[half:], "dp", IN_TO_OUT, f"return_after{i}")
        return done

    def finish(done):
        parts = []
        if "crossed" in done:
            parts.append(add(done["kept"], done["crossed"]))
        if "returned" in done:
            parts.append(jnp.where(is_inner, done["mine"], done["returned"]))
        return parts

    half = own.shape[0] // 2
    hops, seconds = [], []
    for i in range(n):
        if i:
            gates = list(seconds[-1].values()) if i > 1 and i < DEEP else []
            seconds.append(second_hop(i - 1, hops[i - 1], *gates)) if i < DEEP else None
            leaving = [seconds[-1][k] for k in ("kept", "mine") if k in seconds[-1]]
            later = [near[i + 1]] if i + 1 < n else []
            far[i] = after(far[i], *leaving, *later)
            forward(i + 1)
        hop, gate = first_hop(i)
        hops.append(hop)
    for i in range(len(seconds), n):
        gates = list(seconds[-1].values()) if i else []
        seconds.append(second_hop(i, hops[i], gate, *gates))
    quarter = half // 2
    mine, theirs = [], []
    for i, done in enumerate(seconds):
        x = jnp.concatenate(finish(done), axis=1)
        mine.append(jnp.where(is_left, x[:quarter], x[quarter:]))
        theirs.append(
            send(jnp.where(is_left, x[quarter:], x[:quarter]), "tp", CORE, f"rest{i}")
        )
    mine, theirs = jnp.concatenate(mine, axis=1), jnp.concatenate(theirs, axis=1)
    left = jnp.where(is_left, mine, theirs)
    right = jnp.where(is_left, theirs, mine)
    return jnp.concatenate([left, right], axis=1)[None]


def solution(mesh):
    in_specs = (
        P("dp", "ctx", "tp"),
        P("dp", None, "ctx", "tp"),
        P(("dp", "ctx"), None, "tp"),
        P(("dp", "ctx"), None, None, "tp"),
        P(("dp", "ctx"), None),
        P(("dp", "ctx")),
        P(),
        P("tp", "dp", "ctx"),
    )
    out_specs = P("dp", "tp", "ctx")
    return jax.shard_map(local, mesh=mesh, in_specs=in_specs, out_specs=out_specs, check_vma=False)
```

```python
import functools
import math

import jax
import jax.numpy as jnp
from jax import lax
from jax.experimental import pallas as pl
from jax.experimental.pallas import tpu as pltpu
from jax.sharding import PartitionSpec as P

NEGATIVE_FILL = -1e30
ROPE_BASE = 500000.0
COUNT_ROWS = 8
DEEP = 2
FIRST_ROW, BASE, LIVE, CTX, HALVES, PLANE = 0, 1, 3, 4, 5, 7
VMEM_LIMIT = 56 * 1024 * 1024
SMALL_LIMIT = 12 * 1024 * 1024
OUT_TO_IN = [(0, 1), (3, 2)]
IN_TO_OUT = [(1, 0), (2, 3)]
INNER = [(1, 2), (2, 1)]
CORE = [(i, i ^ 1) for i in range(4)]
CROSS = [(i, i ^ 2) for i in range(4)]

SMEM_SPEC = pl.BlockSpec(memory_space=pltpu.SMEM)


def params(rows=0):
    limit = VMEM_LIMIT if rows > 512 else SMALL_LIMIT
    return pltpu.CompilerParams(vmem_limit_bytes=limit)


def send(x, axis, pairs, name):
    with jax.named_scope(name):
        return lax.ppermute(x, axis, pairs)


def after(value, *done):
    return lax.optimization_barrier((value, *done))[0]


def half_turn(x, half):
    return jnp.concatenate([x[:, half:], x[:, :half]], axis=1)


def prepare_kernel(n_blocks, base_ref, doc_ref, rescale_ref, *tables):
    slots = doc_ref.shape[1]
    half = rescale_ref.shape[1]
    head = 2 * half
    rescale = jnp.concatenate([rescale_ref[...], rescale_ref[...]], axis=1)
    lane = lax.broadcasted_iota(jnp.int32, (1, head), 1)
    frequency = jnp.where(lane < half, lane, lane - half).astype(jnp.float32)
    inverse = jnp.exp(-(frequency * (2.0 / head)) * math.log(ROPE_BASE)) / rescale
    sign = jnp.where(lane < half, -1.0, 1.0)
    docs = jnp.broadcast_to(doc_ref[...].astype(jnp.float32), (slots, slots))
    first = jnp.sum(jnp.where(docs < docs.T, 1.0, 0.0), axis=1, keepdims=True)
    slot = lax.broadcasted_iota(jnp.int32, (slots, 1), 0).astype(jnp.float32)
    for i in range(n_blocks + 1):
        cos_ref, sin_ref = tables[2 * i], tables[2 * i + 1]
        if i == n_blocks:
            position = slot - first
        else:
            rows = lax.broadcasted_iota(jnp.int32, (cos_ref.shape[0], 1), 0)
            position = (rows + base_ref[BASE + i]).astype(jnp.float32)
        angles = position * inverse
        cos_ref[...] = jnp.cos(angles)
        sin_ref[...] = jnp.sin(angles) * sign


def prepare(bases, block_rows, doc, rescale):
    vmem = pl.BlockSpec(memory_space=pltpu.VMEM)
    shapes = [
        jax.ShapeDtypeStruct((rows, 2 * rescale.shape[1]), jnp.float32)
        for rows in [*block_rows, doc.shape[1]]
        for _ in range(2)
    ]
    return pl.pallas_call(
        functools.partial(prepare_kernel, len(block_rows)),
        in_specs=[SMEM_SPEC, vmem, vmem],
        out_specs=[vmem] * len(shapes),
        out_shape=shapes,
        compiler_params=params(),
        name="prepare",
    )(bases, doc, rescale)


def weigh(scores, visible, values, scale):
    scores = [jnp.where(v, s, NEGATIVE_FILL) for s, v in zip(scores, visible)]
    peak = functools.reduce(jnp.maximum, [jnp.max(s, axis=1, keepdims=True) for s in scores])
    total, weighted = 0.0, 0.0
    for s, value in zip(scores, values):
        weights = jnp.exp2((s - peak) * (scale * math.log2(math.e)))
        total = total + jnp.sum(weights, axis=1, keepdims=True)
        weighted = weighted + jnp.dot(
            weights.astype(jnp.bfloat16), value, preferred_element_type=jnp.float32
        )
    return (weighted / total).astype(jnp.bfloat16)


def dot_t(a, b):
    return lax.dot_general(a, b, (((1,), (1,)), ((), ())), preferred_element_type=jnp.float32)


def turn(x, cosine, sine):
    x = x.astype(jnp.float32)
    return (x * cosine + half_turn(x, x.shape[1] // 2) * sine).astype(jnp.bfloat16)


def attend_kernel(n_blocks, n_tables, scalar_ref, ql_ref, qs_ref, skv_ref, doc_ref, *rest):
    tables, rest = rest[:n_tables], rest[n_tables:]
    pairs, rest = rest[:n_blocks], rest[n_blocks:]
    out_ref = rest[-1]
    long_rows, slots = ql_ref.shape[0], qs_ref.shape[0]
    head = skv_ref.shape[2]
    scale = 1.0 / math.sqrt(head)
    heads = ql_ref.shape[1] // head
    if n_tables == 2 * n_blocks + 2:
        own_table = (tables[0][...], tables[1][...])
    else:
        own_table = (tables[-4][...], tables[-3][...])
    slab_table = (tables[-2][...], tables[-1][...])
    keys = [turn(p[0], tables[2 * i][...], tables[2 * i + 1][...]) for i, p in enumerate(pairs)]
    values = [p[1] for p in pairs]
    row = lax.broadcasted_iota(jnp.int32, (long_rows, 1), 0) + scalar_ref[FIRST_ROW]
    visible = [
        lax.broadcasted_iota(jnp.int32, (long_rows, p.shape[1]), 1) + scalar_ref[BASE + i] <= row
        for i, p in enumerate(pairs)
    ]
    short_keys = turn(skv_ref[0], *slab_table)
    docs = jnp.broadcast_to(doc_ref[...].astype(jnp.float32), (slots, slots))
    below = lax.broadcasted_iota(jnp.int32, (slots, slots), 1) <= lax.broadcasted_iota(
        jnp.int32, (slots, slots), 0
    )
    short_visible = [(docs == docs.T) & below]
    short_values = [skv_ref[1]]
    for h in range(heads):
        columns = slice(h * head, (h + 1) * head)
        query = turn(ql_ref[:, columns], *own_table)
        scores = [dot_t(query, k) for k in keys]
        out_ref[:long_rows, columns] = weigh(scores, visible, values, scale)
        query = turn(qs_ref[:, columns], *slab_table)
        out_ref[long_rows : long_rows + slots, columns] = weigh(
            [dot_t(query, short_keys)], short_visible, short_values, scale
        )
    live = jnp.full((COUNT_ROWS, out_ref.shape[1]), scalar_ref[LIVE], jnp.int32)
    out_ref[long_rows + slots :, :] = live.astype(jnp.float32).astype(jnp.bfloat16)


def attend(scalars, q_long, q_short, short_kv, doc, tables, pairs):
    rows = q_long.shape[0] + q_short.shape[0] + COUNT_ROWS
    vmem = pl.BlockSpec(memory_space=pltpu.VMEM)
    return pl.pallas_call(
        functools.partial(attend_kernel, len(pairs), len(tables)),
        in_specs=[SMEM_SPEC] + [vmem] * (4 + len(tables) + len(pairs)),
        out_specs=vmem,
        out_shape=jax.ShapeDtypeStruct((rows, q_long.shape[1]), jnp.bfloat16),
        compiler_params=params(sum(p.shape[1] for p in pairs)),
        name="attend",
    )(scalars, q_long, q_short, short_kv, doc, *tables, *pairs)


def pack_kernel(long_rows, slots, group_rows, n_pieces, scalar_ref, *rest):
    pieces, (out_ref, dense) = rest[:-2], rest[-2:]
    piece_rows = long_rows + slots

    def live_of(piece, first):
        tail = piece[pl.ds(first + piece_rows, COUNT_ROWS), :]
        return jnp.max(tail.astype(jnp.float32)).astype(jnp.int32)

    def put(piece, first, offset):
        rows = piece[pl.ds(first, piece_rows), :].astype(jnp.float32)
        dense[pl.ds(pl.multiple_of(offset, 8), piece_rows), :] = rows
        return offset + long_rows + live_of(piece, first)

    if len(pieces) == 1:
        offset = jnp.int32(0)
        for i in range(n_pieces):
            offset = put(pieces[0], i * (piece_rows + COUNT_ROWS), offset)
    else:
        mine, theirs = pieces

        @pl.when(scalar_ref[CTX] == 0)
        def _():
            put(theirs, 0, put(mine, 0, jnp.int32(0)))

        @pl.when(scalar_ref[CTX] != 0)
        def _():
            put(mine, 0, put(theirs, 0, jnp.int32(0)))

    half = group_rows // 2
    for s in range(2):
        start = pl.multiple_of(scalar_ref[HALVES + s] * half, 8)
        out_ref[s * half : (s + 1) * half, :] = dense[pl.ds(start, half), :].astype(jnp.bfloat16)


def pack(place, pieces, long_rows, slots, n_pieces):
    group_rows = n_pieces * (long_rows + 3 * slots // 4)
    columns = pieces[0].shape[1]
    block = min(columns, 512 if n_pieces == 2 else 256)
    return pl.pallas_call(
        functools.partial(pack_kernel, long_rows, slots, group_rows, n_pieces),
        grid_spec=pltpu.PrefetchScalarGridSpec(
            num_scalar_prefetch=1,
            grid=(columns // block,),
            in_specs=[pl.BlockSpec((p.shape[0], block), lambda j, s: (0, j)) for p in pieces],
            out_specs=pl.BlockSpec((group_rows, block), lambda j, s: (0, j)),
            scratch_shapes=[pltpu.VMEM((group_rows + long_rows + slots, block), jnp.float32)],
        ),
        out_shape=jax.ShapeDtypeStruct((group_rows, columns), jnp.bfloat16),
        compiler_params=params(group_rows // 2),
        name="pack",
    )(place, *pieces)


def project_kernel(at, width, straight, plane_ref, *refs):
    pieces = 2 if straight < width else 1
    count = 2 * pieces + 2
    rows, weights, outs = refs[:4], refs[4 : 4 + count], refs[4 + count :]
    depth = weights[0].shape[0] // 2
    half = rows[0].shape[0] // 2

    def block(i, part, a, b):
        here = slice(part * depth, (part + 1) * depth)
        if i > 1:
            return weights[2 * pieces + i - 2][here, a:b]
        sides, first = [], 0
        for ref in weights[i * pieces : (i + 1) * pieces]:
            x, y = max(at + a, first), min(at + b, first + ref.shape[1])
            if x < y:
                sides.append(ref[here, x - first : y - first])
            first += ref.shape[1]
        return sides[0] if len(sides) == 1 else jnp.concatenate(sides, axis=1)

    for plane, order in ((1, (2, 0, 1, 3)), (2, (3, 1, 0, 2))):

        @pl.when(plane_ref[PLANE] == plane)
        def _(order=order):
            for first in range(0, width, 512):
                last = min(width, first + 512)
                for bounds in ((first, min(last, straight)), (max(first, straight), last)):
                    a, b = bounds
                    if a >= b:
                        continue
                    weight = jnp.concatenate(
                        [block(i, part, a, b) for part in range(2) for i in order], axis=0
                    )
                    for group in range(2):
                        left = jnp.concatenate([rows[2 * group][...], rows[2 * group + 1][...]], axis=1)
                        total = jnp.dot(left, weight, preferred_element_type=jnp.float32)
                        total = total.astype(jnp.bfloat16)
                        if b <= straight:
                            outs[group][:, a:b] = total
                        else:
                            here = slice(a - straight, b - straight)
                            there = slice(group * half, (group + 1) * half)
                            outs[-2][there, here] = total[:half]
                            outs[-1][there, here] = total[half:]

    @pl.when((plane_ref[PLANE] != 1) & (plane_ref[PLANE] != 2))
    def _():
        for out in outs:
            out[...] = jnp.zeros(out.shape, jnp.bfloat16)


def project(plane, rows, weights, at, width, straight):
    count = rows[0].shape[0]
    vmem = pl.BlockSpec(memory_space=pltpu.VMEM)
    shapes = [jax.ShapeDtypeStruct((count, w), jnp.bfloat16) for w in (straight, width - straight) if w for _ in range(2)]
    grid, row_spec, out_spec = (), vmem, vmem
    if count > 1024 and width == straight:
        block = count // 8
        grid = (8,)
        row_spec = pl.BlockSpec((block, rows[0].shape[1]), lambda i: (i, 0))
        out_spec = pl.BlockSpec((block, width), lambda i: (i, 0))
    return pl.pallas_call(
        functools.partial(project_kernel, at, width, straight),
        grid=grid,
        in_specs=[SMEM_SPEC] + [row_spec] * 4 + [vmem] * len(weights),
        out_specs=[out_spec] * len(shapes),
        out_shape=shapes,
        compiler_params=params(count // 2),
        name="project",
    )(plane, *rows, *weights)


def column_chunks(columns):
    unit = columns // 16
    if unit % 128:
        return [columns], [columns]
    return [4 * unit, 6 * unit, 6 * unit], [2 * unit, 3 * unit, 3 * unit]


def local(
    q_long, long_key_value, q_short, short_key_value, doc_ids, live_counts, rescale, output_weight
):
    head = rescale.shape[0] * 2
    long_rows, slots = q_long.shape[1], q_short.shape[1]
    ctx, tp, dp = lax.axis_index("ctx"), lax.axis_index("tp"), lax.axis_index("dp")
    n_ctx = lax.axis_size("ctx")
    own_base = ctx * long_rows
    bases = [own_base, (1 - ctx) * long_rows] if n_ctx == 2 else [jnp.int32(0), own_base]
    place = jnp.stack(
        [own_base, *bases, live_counts[0], ctx, 1 - (tp >> 1), tp >> 1, dp]
    ).astype(jnp.int32)
    weight = output_weight[0]
    width = weight.shape[1] // 2
    place, is_inner, is_left, keep_at, give_at, weight, factors = lax.optimization_barrier(
        (
            place,
            (dp == 1) | (dp == 2),
            (tp & 1) == 0,
            (tp & 1) * width,
            (1 - (tp & 1)) * width,
            weight,
            rescale.reshape(1, head // 2),
        )
    )

    def swap_ctx(x, name):
        return send(x, "ctx", [(0, 1), (1, 0)], name)

    widths, straight = column_chunks(width)
    n = len(widths)
    given = lax.dynamic_slice_in_dim(weight, give_at, width, 1)
    kept = lax.dynamic_slice_in_dim(weight, keep_at, width, 1)

    def trade(a, b, name):
        theirs = send(given[:, a:b], "tp", CORE, name)
        return jnp.concatenate([kept[:, a:b], theirs], axis=0)

    near, far = {}, {}
    cut = width // 2 if n > 1 else width
    both = [trade(0, cut, "trade0")]
    columns = [sum(widths[:i]) for i in range(n)]

    def fetch_near(i, *gates):
        if i < n:
            a, b = columns[i], columns[i] + widths[i]
            sides = []
            if a < cut:
                sides.append(both[0][:, a : min(b, cut)])
            if b > cut:
                sides.append(both[1][:, max(a, cut) - cut : b - cut])
            source = sides[0] if len(sides) == 1 else jnp.concatenate(sides, axis=1)
            near[i] = send(after(source, *gates), "dp", OUT_TO_IN, f"near{i}")

    fetch_near(0, place)
    twin = [send(both[0], "dp", INNER, "twin0")]
    if n > 1:
        both.append(trade(cut, width, "trade1"))

    def forward(i, *gates):
        if i < n:
            far[i] = send(after(near[i], *gates), "dp", INNER, f"far{i}")

    raw = long_key_value[0]
    if n_ctx == 2:
        pairs = [raw, swap_ctx(raw, "keys")]
        block_rows = [long_rows, long_rows]
    else:
        pairs = [lax.all_gather(raw, "ctx", axis=1, tiled=True)]
        block_rows = [n_ctx * long_rows, long_rows]
    tables = prepare(place, block_rows, doc_ids, factors)
    inputs = (place, q_long[0], q_short[0], short_key_value[0], doc_ids, tables, pairs)
    if n > 1:
        inputs = (after(place, both[1]), *inputs[1:])
    rows = attend(*inputs)
    forward(0, rows)
    rows = after(rows, near[0])

    def gathered(x, name):
        if n_ctx == 2:
            return [x, swap_ctx(x, name)]
        return [lax.all_gather(x, "ctx", axis=0, tiled=True)]

    handed = send(rows, "dp", OUT_TO_IN, "hand")
    pieces = gathered(rows, "rows")
    other_pieces = gathered(handed, "other")
    if n > 1:
        twin.append(send(after(both[1], handed, twin[0]), "dp", INNER, "twin1"))
    fetch_near(1, handed, twin[0])
    pieces[-1] = after(pieces[-1], handed, far[0], twin[0])
    own = pack(place, pieces, long_rows, slots, n_ctx)
    own_theirs = send(own, "tp", CORE, "own_rows")
    if n > 1:
        other_pieces[-1] = after(other_pieces[-1], near[1], own_theirs, twin[1])
    other = pack(place, other_pieces, long_rows, slots, n_ctx)
    other_theirs = send(other, "tp", CORE, "other_rows")
    forward(1, other)
    fetch_near(2, other)
    group = (own, own_theirs, other, other_theirs)

    def add(a, b):
        return (a.astype(jnp.float32) + b.astype(jnp.float32)).astype(jnp.bfloat16)

    def first_hop(i):
        outs = project(
            place, group, (*both, *twin, near[i], far[i]), columns[i], widths[i], straight[i]
        )
        hop = {}
        if straight[i]:
            hop["mine"], other_part = outs[0], outs[1]
            hop["returned"] = send(other_part, "dp", IN_TO_OUT, f"return{i}")
        if straight[i] < widths[i]:
            hop["kept"] = outs[-1]
            hop["crossed"] = send(outs[-2], "tp", CROSS, f"cross{i}")
        return hop, outs[0]

    def second_hop(i, hop, *gates):
        done = {}
        if "returned" in hop:
            summed = jnp.where(is_inner, hop["mine"], after(hop["returned"], *gates))
            done["kept"] = summed[half:]
            done["crossed"] = send(summed[:half], "tp", CROSS, f"cross_after{i}")
        if "crossed" in hop:
            summed = add(hop["kept"], after(hop["crossed"], *gates))
            done["mine"] = summed[:half]
            done["returned"] = send(summed[half:], "dp", IN_TO_OUT, f"return_after{i}")
        return done

    def finish(done):
        parts = []
        if "crossed" in done:
            parts.append(add(done["kept"], done["crossed"]))
        if "returned" in done:
            parts.append(jnp.where(is_inner, done["mine"], done["returned"]))
        return parts

    half = own.shape[0] // 2
    hops, seconds = [], []
    for i in range(n):
        if i:
            gates = list(seconds[-1].values()) if i > 1 and i < DEEP else []
            seconds.append(second_hop(i - 1, hops[i - 1], *gates)) if i < DEEP else None
            leaving = [seconds[-1][k] for k in ("kept", "mine") if k in seconds[-1]]
            later = [near[i + 1]] if i + 1 < n else []
            far[i] = after(far[i], *leaving, *later, *([gate] if i > 1 else []))
            forward(i + 1)
        hop, gate = first_hop(i)
        hops.append(hop)
    for i in range(len(seconds), n):
        gates = [v for k, v in seconds[-1].items() if k in ("kept", "mine")] if i else []
        seconds.append(second_hop(i, hops[i], gate, *gates))
    quarter = half // 2
    mine, theirs = [], []
    for i, done in enumerate(seconds):
        x = jnp.concatenate(finish(done), axis=1)
        mine.append(jnp.where(is_left, x[:quarter], x[quarter:]))
        theirs.append(
            send(jnp.where(is_left, x[quarter:], x[:quarter]), "tp", CORE, f"rest{i}")
        )
    mine, theirs = jnp.concatenate(mine, axis=1), jnp.concatenate(theirs, axis=1)
    left = jnp.where(is_left, mine, theirs)
    right = jnp.where(is_left, theirs, mine)
    return jnp.concatenate([left, right], axis=1)[None]


def solution(mesh):
    in_specs = (
        P("dp", "ctx", "tp"),
        P("dp", None, "ctx", "tp"),
        P(("dp", "ctx"), None, "tp"),
        P(("dp", "ctx"), None, None, "tp"),
        P(("dp", "ctx"), None),
        P(("dp", "ctx")),
        P(),
        P("tp", "dp", "ctx"),
    )
    out_specs = P("dp", "tp", "ctx")
    return jax.shard_map(local, mesh=mesh, in_specs=in_specs, out_specs=out_specs, check_vma=False)
```
